256 devices in a mesh: rows: 32 (over z, y), cols: 8 (over x, core).
Axes of the slice: x: 4, y: 4, z: 8, core: 2. Of those that a mesh axis runs over, the one named last changes fastest.
Arguments:
- features: bfloat16 [384, 1280, 256], P('rows', 'cols'), may hold values from -6 to 6
- weight: bfloat16 [3, 3, 256, 128], replicated, may hold values from -0.125 to 0.125
- cotangent: bfloat16 [384, 1280, 128], P('rows', 'cols'), may hold values from -6 to 6
Outputs:
- conv_out: bfloat16 [384, 1280, 128], P('rows', 'cols')
- input_grad: bfloat16 [384, 1280, 256], P('rows', 'cols')
- weight_grad: float32 [3, 3, 256, 128], replicated
The draws below stay inside these ranges and needn't reach their ends.
All inputs are finite; a program needn't handle non-finite values.
Results may differ from the reference program's by a relative error of at most 0.001.
Values may be sent and summed in bfloat16 or wider, within the bound.
A program may use at most 64 MiB of HBM per device.

```python
import jax
import jax.numpy as jnp

CIN = 256
COUT = 128
DILATION_STEP = 12
HEIGHT = 384
WIDTH = 1280


def levels(stream_key, extent, pieces, least, largest):
    loudness, own = 1.0, jax.random.fold_in(stream_key, 6)
    for position, parts in pieces:
        draws = jnp.exp(jax.random.uniform(jax.random.fold_in(own, position), (parts,), jnp.float32, least / len(pieces), largest / len(pieces)))
        loudness = loudness * jnp.repeat(draws, extent[position] // parts).reshape([-1 if axis == position else 1 for axis in range(len(extent))])
    return loudness


def normal_values(rng, dims, deviation, most, cuts=(), kind=jnp.bfloat16):
    values = deviation * jax.random.normal(rng, dims, jnp.float32)
    if cuts:
        values = values * levels(rng, dims, cuts, -0.22, 0.18)
    return jnp.clip(values, -most, most).astype(kind)


def setup_inputs(seed: int = 0) -> dict:
    key_of = jax.random.split(jax.random.key(seed), 4)
    features = normal_values(key_of[0], (HEIGHT, WIDTH, CIN), 1.0, 6.0, ((0, 32), (1, 8)))
    weight = normal_values(key_of[1], (3, 3, CIN, COUT), (9 * CIN) ** -0.5, 0.125)
    cotangent = normal_values(key_of[2], (HEIGHT, WIDTH, COUT), 1.0, 6.0, ((0, 32), (1, 8)))
    return {"features": features, "weight": weight, "cotangent": cotangent}


def window(border_padded, row_offset_tap, column_offset_tap, map_height, map_width):
    return border_padded[DILATION_STEP * row_offset_tap:DILATION_STEP * row_offset_tap + map_height, DILATION_STEP * column_offset_tap:DILATION_STEP * column_offset_tap + map_width]

def reference(features, weight, cotangent):
    map_height, map_width = (features.shape[0], features.shape[1])
    cin, cout = (weight.shape[2], weight.shape[3])
    padded_feature_map = jnp.pad(features, ((DILATION_STEP, DILATION_STEP), (DILATION_STEP, DILATION_STEP), (0, 0)))
    padded_gradient_map = jnp.pad(cotangent, ((DILATION_STEP, DILATION_STEP), (DILATION_STEP, DILATION_STEP), (0, 0)))
    flat_grad = cotangent.reshape(map_height * map_width, cout)
    output = jnp.zeros((map_height * map_width, cout), jnp.float32)
    back = jnp.zeros((map_height * map_width, cin), jnp.float32)
    kernels = []
    for row_offset_tap in range(3):
        for column_offset_tap in range(3):
            tap_weight = weight[row_offset_tap, column_offset_tap]
            piece = window(padded_feature_map, row_offset_tap, column_offset_tap, map_height, map_width).reshape(map_height * map_width, cin)
            output = output + jnp.dot(piece, tap_weight, preferred_element_type=jnp.float32)
            gpiece = window(padded_gradient_map, 2 - row_offset_tap, 2 - column_offset_tap, map_height, map_width).reshape(map_height * map_width, cout)
            back = back + jnp.dot(gpiece, tap_weight.T, preferred_element_type=jnp.float32)
            kernels.append(jnp.dot(piece.T, flat_grad, preferred_element_type=jnp.float32))
    scale = 1.0 / jnp.sqrt(jnp.float32(map_height * map_width))
    weight_grad = jnp.stack(kernels).reshape(3, 3, cin, cout) * scale
    conv_out = output.reshape(map_height, map_width, cout).astype(jnp.bfloat16)
    input_grad = back.reshape(map_height, map_width, cin).astype(jnp.bfloat16)
    return (conv_out, input_grad, weight_grad)
```

```python
import functools

import jax
import jax.numpy as jnp
from jax import lax
from jax.experimental import pallas as pl
from jax.experimental.pallas import tpu as pltpu
from jax.sharding import PartitionSpec as P

DILATION_STEP = 12
MESH = pl.DeviceIdType.MESH
NX, NY, NZ = 4, 4, 8
HALF, SHARD, PART = 384, 96, 16


def position():
    row, col = lax.axis_index("rows"), lax.axis_index("cols")
    return row, col, lax.div(col, 2), lax.rem(col, 2), lax.rem(row, NY), lax.div(row, NY)


def z_offset(z):
    return pl.multiple_of(lax.div(3 * z, 2) * 8, 8)


def rows_at(start, size):
    return pl.ds(pl.multiple_of(start, 8), size)


class Reduction:
    def __init__(self, piece, where, partial, total, scratch):
        self.k = piece
        self.row, self.col, self.x, self.core, self.y, self.z = where
        (self.half, self.s1, self.xs, self.s2, self.zs, self.ys, self.zg, self.xg_own, self.near, self.xsem, self.zsem, self.ysem,
         self.zgsem, self.xgsem, self.farsem) = scratch
        self.partial, self.total = partial, total

    def copy(self, src, dst, sems, to):
        return pltpu.make_async_remote_copy(
            src_ref=src, dst_ref=dst, send_sem=sems[0], recv_sem=sems[1], device_id=to, device_id_type=MESH
        )

    def partner(self):
        return (self.row, self.x * 2 + 1 - self.core)

    def x_peer(self, d):
        return (self.row, lax.rem(self.x + d, NX) * 2 + self.core)

    def y_peer(self, d):
        return (self.z * NY + lax.rem(self.y + d, NY), self.col)

    def z_peer(self, d):
        return (lax.rem(self.z + d, NZ) * NY + self.y, self.col)

    def core_copy(self):
        k = self.k
        return self.copy(
            self.partial.at[k, rows_at((1 - self.core) * HALF, HALF)], self.half.at[k], (self.near.at[0, k], self.near.at[1, k]),
            self.partner(),
        )

    def x_copy(self, d):
        k = self.k
        target = lax.rem(self.x + d, NX)
        return self.copy(
            self.s1.at[k, rows_at(target * SHARD, SHARD)], self.xs.at[k, d - 1], (self.xsem.at[0, k, d - 1], self.xsem.at[1, k, d - 1]),
            self.x_peer(d),
        )

    def z_copy(self, d):
        k = self.k
        target = lax.rem(self.z + d, NZ)
        return self.copy(
            self.s2.at[k, pl.ds(z_offset(target), PART)], self.zs.at[k, d - 1], (self.zsem.at[0, k, d - 1], self.zsem.at[1, k, d - 1]),
            self.z_peer(d),
        )

    def y_copy(self, d):
        k = self.k
        return self.copy(
            self.ys.at[k, self.y], self.ys.at[k, self.y], (self.ysem.at[0, k, d - 1], self.ysem.at[1, k, d - 1]), self.y_peer(d)
        )

    def zg_copy(self, d):
        k = self.k
        return self.copy(
            self.zg.at[k, self.z], self.zg.at[k, self.z], (self.zgsem.at[0, k, d - 1], self.zgsem.at[1, k, d - 1]), self.z_peer(d)
        )

    def span(self, x):
        return rows_at(self.core * HALF + x * SHARD, SHARD)

    def xg_copy(self, d):
        k = self.k
        return self.copy(
            self.total.at[k, self.span(self.x)], self.total.at[k, self.span(self.x)],
            (self.xgsem.at[0, k, d - 1], self.xgsem.at[1, k, d - 1]), self.x_peer(d),
        )

    def far_copy(self, d):
        k = self.k
        span = self.span(lax.rem(self.x + NX - d, NX))
        return self.copy(
            self.total.at[k, span], self.total.at[k, span], (self.farsem.at[0, k, d], self.farsem.at[1, k, d]), self.partner()
        )

    def loop(self, n, body):
        def step(d, carry):
            body(d)
            return carry

        lax.fori_loop(1, n, step, 0)

    def to_core(self):
        self.core_copy().start()

    def to_x(self):
        k = self.k
        self.core_copy().wait_recv()
        self.s1[k] = self.partial[k, rows_at(self.core * HALF, HALF)] + self.half[k]
        for d in (1, 3, 2):
            self.x_copy(d).start()

    def to_z(self):
        k = self.k
        for d in range(1, NX):
            self.x_copy(d).wait_recv()
        self.s2[k] = self.s1[k, rows_at(self.x * SHARD, SHARD)] + self.xs[k, 0] + self.xs[k, 1] + self.xs[k, 2]
        self.loop(NZ, lambda d: self.z_copy(d).start())

    def to_y(self):
        k = self.k
        self.loop(NZ, lambda d: self.z_copy(d).wait_recv())
        mine = self.s2[k, pl.ds(z_offset(self.z), PART)]
        for d in range(NZ - 1):
            mine = mine + self.zs[k, d]
        self.ys[k, self.y] = mine
        for d in range(1, NY):
            self.y_copy(d).start()

    def gather_z(self, scale):
        k = self.k
        for d in range(1, NY):
            self.y_copy(d).wait_recv()
        self.zg[k, self.z] = (self.ys[k, 0] + self.ys[k, 1] + self.ys[k, 2] + self.ys[k, 3]) * scale
        self.loop(NZ, lambda d: self.zg_copy(d).start())

    def gather_x(self):
        k = self.k
        self.loop(NZ, lambda d: self.zg_copy(d).wait_recv())
        base = self.core * HALF + self.x * SHARD
        for pair in range(NZ // 2):
            self.total[k, rows_at(base + 24 * pair, 16)] = self.zg[k, 2 * pair]
            self.total[k, rows_at(base + 24 * pair + 16, 8)] = self.zg[k, 2 * pair + 1, 8:16]
        for d in (1, 3, 2):
            self.xg_copy(d).start()
        self.far_copy(0).start()

    def gather_core(self):
        for d in (1, 3, 2):
            self.xg_copy(d).wait_recv()
            self.far_copy(d).start()

    def finish(self):
        for d in range(NX):
            self.far_copy(d).wait_recv()

    def drain(self):
        self.core_copy().wait_send()
        for d in range(1, NX):
            self.x_copy(d).wait_send()
            self.xg_copy(d).wait_send()
        self.loop(NZ, lambda d: self.z_copy(d).wait_send())
        self.loop(NZ, lambda d: self.zg_copy(d).wait_send())
        for d in range(1, NY):
            self.y_copy(d).wait_send()
        for d in range(NX):
            self.far_copy(d).wait_send()


def reduction_scratch(pieces):
    f32 = jnp.float32
    dma = pltpu.SemaphoreType.DMA
    return [
        pltpu.VMEM((pieces, HALF, 128), f32),
        pltpu.VMEM((pieces, HALF, 128), f32),
        pltpu.VMEM((pieces, NX - 1, SHARD, 128), f32),
        pltpu.VMEM((pieces, SHARD, 128), f32),
        pltpu.VMEM((pieces, NZ - 1, PART, 128), f32),
        pltpu.VMEM((pieces, NY, PART, 128), f32),
        pltpu.VMEM((pieces, NZ, PART, 128), f32),
        pltpu.VMEM((8, 128), f32),
        dma((2, pieces)),
        dma((2, pieces, NX - 1)),
        dma((2, pieces, NZ - 1)),
        dma((2, pieces, NY - 1)),
        dma((2, pieces, NZ - 1)),
        dma((2, pieces, NX - 1)),
        dma((2, pieces, NX)),
    ]


def greet(where, extra=()):
    row, col, x, core, y, z = where
    barrier = pltpu.get_barrier_semaphore()

    def signal(to):
        pl.semaphore_signal(barrier, inc=1, device_id=to, device_id_type=MESH)

    count = 0
    for to in extra:
        signal(to)
        count += 1
    signal((row, x * 2 + 1 - core))
    for d in range(1, NX):
        signal((row, lax.rem(x + d, NX) * 2 + core))
    for d in range(1, NY):
        signal((z * NY + lax.rem(y + d, NY), col))

    def step(d, carry):
        signal((lax.rem(z + d, NZ) * NY + y, col))
        return carry

    lax.fori_loop(1, NZ, step, 0)
    pl.semaphore_wait(barrier, count + 1 + NX - 1 + NY - 1 + NZ - 1)


def reduce_kernel(scale, partial, total, *scratch):
    where = position()
    greet(where)
    pieces = [Reduction(k, where, partial, total, scratch) for k in range(3)]
    for p in pieces:
        p.to_core()
    for p in pieces:
        p.to_x()
    for p in pieces:
        p.to_z()
    for p in pieces:
        p.to_y()
    for p in pieces:
        p.gather_z(scale)
    for p in pieces:
        p.gather_x()
    for p in pieces:
        p.gather_core()
    for p in pieces:
        p.finish()
    for p in pieces:
        p.drain()


def reduced(partial, scale):
    return pl.pallas_call(
        functools.partial(reduce_kernel, scale),
        out_shape=jax.ShapeDtypeStruct((3, 768, 128), jnp.float32),
        in_specs=[pl.BlockSpec(memory_space=pltpu.VMEM)],
        out_specs=pl.BlockSpec(memory_space=pltpu.VMEM),
        scratch_shapes=reduction_scratch(3),
        compiler_params=pltpu.CompilerParams(collective_id=0, has_side_effects=True),
        name="reduce_kernel",
    )(partial)


def extended(cells, sides, width):
    for axis, dim in sides:
        count = lax.axis_size(axis)
        ends = count - 1
        head = lax.slice_in_dim(cells, 0, width, axis=dim)
        tail = lax.slice_in_dim(cells, cells.shape[dim] - width, cells.shape[dim], axis=dim)
        cells = jnp.concatenate(
            [
                lax.ppermute(tail, axis, [(i, (i + 1) % count) for i in range(ends)]),
                cells,
                lax.ppermute(head, axis, [((i + 1) % count, i) for i in range(ends)]),
            ],
            axis=dim,
        )
    return cells


def window(border_padded, row_offset_tap, column_offset_tap, map_height, map_width):
    return border_padded[
        DILATION_STEP * row_offset_tap : DILATION_STEP * row_offset_tap + map_height,
        DILATION_STEP * column_offset_tap : DILATION_STEP * column_offset_tap + map_width,
    ]


def body(features, weight, cotangent):
    map_height, map_width = (features.shape[0], features.shape[1])
    cin, cout = (weight.shape[2], weight.shape[3])
    padded_feature_map = extended(features, (("rows", 0), ("cols", 1)), DILATION_STEP)
    padded_gradient_map = extended(cotangent, (("rows", 0), ("cols", 1)), DILATION_STEP)
    flat_grad = cotangent.reshape(map_height * map_width, cout)
    output = jnp.zeros((map_height * map_width, cout), jnp.float32)
    back = jnp.zeros((map_height * map_width, cin), jnp.float32)
    kernels = []
    for row_offset_tap in range(3):
        for column_offset_tap in range(3):
            tap_weight = weight[row_offset_tap, column_offset_tap]
            piece = window(
                padded_feature_map, row_offset_tap, column_offset_tap, map_height, map_width
            ).reshape(map_height * map_width, cin)
            output = output + jnp.dot(piece, tap_weight, preferred_element_type=jnp.float32)
            gpiece = window(
                padded_gradient_map,
                2 - row_offset_tap,
                2 - column_offset_tap,
                map_height,
                map_width,
            ).reshape(map_height * map_width, cout)
            back = back + jnp.dot(gpiece, tap_weight.T, preferred_element_type=jnp.float32)
            kernels.append(jnp.dot(piece.T, flat_grad, preferred_element_type=jnp.float32))
    partial_kernel = jnp.stack(kernels).reshape(3, 3 * cin, cout)
    pixels = map_height * lax.axis_size("rows") * map_width * lax.axis_size("cols")
    weight_grad = reduced(partial_kernel, float(pixels) ** -0.5).reshape(3, 3, cin, cout)
    conv_out = output.reshape(map_height, map_width, cout).astype(jnp.bfloat16)
    input_grad = back.reshape(map_height, map_width, cin).astype(jnp.bfloat16)
    return (conv_out, input_grad, weight_grad)


def solution(mesh):
    placed = (P("rows", "cols", None), P(), P("rows", "cols", None))
    return jax.shard_map(
        body,
        mesh=mesh,
        in_specs=placed,
        out_specs=(P("rows", "cols", None), P("rows", "cols", None), P()),
        check_vma=False,
    )
```

```python
import functools

import jax
import jax.numpy as jnp
from jax import lax
from jax.experimental import pallas as pl
from jax.experimental.pallas import tpu as pltpu
from jax.sharding import PartitionSpec as P

ROWS = 12
BLOCKS, COLS = 32, 8
F_CHUNKS, G_CHUNKS = 4, 2
MESH = pl.DeviceIdType.MESH
NX, NY, NZ = 4, 4, 8
HALF, SHARD, PART = 384, 96, 16


def position():
    row, col = lax.axis_index("rows"), lax.axis_index("cols")
    return row, col, lax.div(col, 2), lax.rem(col, 2), lax.rem(row, NY), lax.div(row, NY)


def z_offset(z):
    return pl.multiple_of(lax.div(3 * z, 2) * 8, 8)


def rows_at(start, size):
    return pl.ds(pl.multiple_of(start, 8), size)


class Reduction:
    def __init__(self, piece, where, partial, total, scratch):
        self.k = piece
        self.row, self.col, self.x, self.core, self.y, self.z = where
        (self.half, self.s1, self.xs, self.s2, self.zs, self.ys, self.zg, self.xg_own, self.near, self.xsem, self.zsem, self.ysem,
         self.zgsem, self.xgsem, self.farsem) = scratch
        self.partial, self.total = partial, total

    def copy(self, src, dst, sems, to):
        return pltpu.make_async_remote_copy(
            src_ref=src, dst_ref=dst, send_sem=sems[0], recv_sem=sems[1], device_id=to, device_id_type=MESH
        )

    def partner(self):
        return (self.row, self.x * 2 + 1 - self.core)

    def x_peer(self, d):
        return (self.row, lax.rem(self.x + d, NX) * 2 + self.core)

    def y_peer(self, d):
        return (self.z * NY + lax.rem(self.y + d, NY), self.col)

    def z_peer(self, d):
        return (lax.rem(self.z + d, NZ) * NY + self.y, self.col)

    def core_copy(self):
        k = self.k
        return self.copy(
            self.partial.at[k, rows_at((1 - self.core) * HALF, HALF)], self.half.at[k], (self.near.at[0, k], self.near.at[1, k]),
            self.partner(),
        )

    def x_copy(self, d):
        k = self.k
        target = lax.rem(self.x + d, NX)
        return self.copy(
            self.s1.at[k, rows_at(target * SHARD, SHARD)], self.xs.at[k, d - 1], (self.xsem.at[0, k, d - 1], self.xsem.at[1, k, d - 1]),
            self.x_peer(d),
        )

    def z_copy(self, d):
        k = self.k
        target = lax.rem(self.z + d, NZ)
        return self.copy(
            self.s2.at[k, pl.ds(z_offset(target), PART)], self.zs.at[k, d - 1], (self.zsem.at[0, k, d - 1], self.zsem.at[1, k, d - 1]),
            self.z_peer(d),
        )

    def y_copy(self, d):
        k = self.k
        return self.copy(
            self.ys.at[k, self.y], self.ys.at[k, self.y], (self.ysem.at[0, k, d - 1], self.ysem.at[1, k, d - 1]), self.y_peer(d)
        )

    def zg_copy(self, d):
        k = self.k
        return self.copy(
            self.zg.at[k, self.z], self.zg.at[k, self.z], (self.zgsem.at[0, k, d - 1], self.zgsem.at[1, k, d - 1]), self.z_peer(d)
        )

    def span(self, x):
        return rows_at(self.core * HALF + x * SHARD, SHARD)

    def xg_copy(self, d):
        k = self.k
        return self.copy(
            self.total.at[k, self.span(self.x)], self.total.at[k, self.span(self.x)],
            (self.xgsem.at[0, k, d - 1], self.xgsem.at[1, k, d - 1]), self.x_peer(d),
        )

    def far_copy(self, d):
        k = self.k
        span = self.span(lax.rem(self.x + NX - d, NX))
        return self.copy(
            self.total.at[k, span], self.total.at[k, span], (self.farsem.at[0, k, d], self.farsem.at[1, k, d]), self.partner()
        )

    def loop(self, n, body):
        def step(d, carry):
            body(d)
            return carry

        lax.fori_loop(1, n, step, 0)

    def to_core(self):
        self.core_copy().start()

    def to_x(self):
        k = self.k
        self.core_copy().wait_recv()
        self.s1[k] = self.partial[k, rows_at(self.core * HALF, HALF)] + self.half[k]
        for d in (1, 3, 2):
            self.x_copy(d).start()

    def to_z(self):
        k = self.k
        for d in range(1, NX):
            self.x_copy(d).wait_recv()
        self.s2[k] = self.s1[k, rows_at(self.x * SHARD, SHARD)] + self.xs[k, 0] + self.xs[k, 1] + self.xs[k, 2]
        self.loop(NZ, lambda d: self.z_copy(d).start())

    def to_y(self):
        k = self.k
        self.loop(NZ, lambda d: self.z_copy(d).wait_recv())
        mine = self.s2[k, pl.ds(z_offset(self.z), PART)]
        for d in range(NZ - 1):
            mine = mine + self.zs[k, d]
        self.ys[k, self.y] = mine
        for d in range(1, NY):
            self.y_copy(d).start()

    def gather_z(self, scale):
        k = self.k
        for d in range(1, NY):
            self.y_copy(d).wait_recv()
        self.zg[k, self.z] = (self.ys[k, 0] + self.ys[k, 1] + self.ys[k, 2] + self.ys[k, 3]) * scale
        self.loop(NZ, lambda d: self.zg_copy(d).start())

    def gather_x(self):
        k = self.k
        self.loop(NZ, lambda d: self.zg_copy(d).wait_recv())
        base = self.core * HALF + self.x * SHARD
        for pair in range(NZ // 2):
            self.total[k, rows_at(base + 24 * pair, 16)] = self.zg[k, 2 * pair]
            self.total[k, rows_at(base + 24 * pair + 16, 8)] = self.zg[k, 2 * pair + 1, 8:16]
        for d in (1, 3, 2):
            self.xg_copy(d).start()
        self.far_copy(0).start()

    def gather_core(self):
        for d in (1, 3, 2):
            self.xg_copy(d).wait_recv()
            self.far_copy(d).start()

    def finish(self):
        for d in range(NX):
            self.far_copy(d).wait_recv()

    def drain(self):
        self.core_copy().wait_send()
        for d in range(1, NX):
            self.x_copy(d).wait_send()
            self.xg_copy(d).wait_send()
        self.loop(NZ, lambda d: self.z_copy(d).wait_send())
        self.loop(NZ, lambda d: self.zg_copy(d).wait_send())
        for d in range(1, NY):
            self.y_copy(d).wait_send()
        for d in range(NX):
            self.far_copy(d).wait_send()


def reduction_scratch(pieces):
    f32 = jnp.float32
    dma = pltpu.SemaphoreType.DMA
    return [
        pltpu.VMEM((pieces, HALF, 128), f32),
        pltpu.VMEM((pieces, HALF, 128), f32),
        pltpu.VMEM((pieces, NX - 1, SHARD, 128), f32),
        pltpu.VMEM((pieces, SHARD, 128), f32),
        pltpu.VMEM((pieces, NZ - 1, PART, 128), f32),
        pltpu.VMEM((pieces, NY, PART, 128), f32),
        pltpu.VMEM((pieces, NZ, PART, 128), f32),
        pltpu.VMEM((8, 128), f32),
        dma((2, pieces)),
        dma((2, pieces, NX - 1)),
        dma((2, pieces, NZ - 1)),
        dma((2, pieces, NY - 1)),
        dma((2, pieces, NZ - 1)),
        dma((2, pieces, NX - 1)),
        dma((2, pieces, NX)),
    ]


def greet(where, extra=()):
    row, col, x, core, y, z = where
    barrier = pltpu.get_barrier_semaphore()

    def signal(to):
        pl.semaphore_signal(barrier, inc=1, device_id=to, device_id_type=MESH)

    count = 0
    for to in extra:
        signal(to)
        count += 1
    signal((row, x * 2 + 1 - core))
    for d in range(1, NX):
        signal((row, lax.rem(x + d, NX) * 2 + core))
    for d in range(1, NY):
        signal((z * NY + lax.rem(y + d, NY), col))

    def step(d, carry):
        signal((lax.rem(z + d, NZ) * NY + y, col))
        return carry

    lax.fori_loop(1, NZ, step, 0)
    pl.semaphore_wait(barrier, count + 1 + NX - 1 + NY - 1 + NZ - 1)


class Halo:
    def __init__(self, buf, where, strip_sem, row_sem, relay_sem, chunks):
        self.buf = buf
        self.row, self.col = where[0], where[1]
        self.strip_sem, self.row_sem, self.relay_sem = strip_sem, row_sem, relay_sem
        self.chunks = chunks
        self.n = ROWS // chunks

    def beside(self, side):
        step = 1 if side == 1 else COLS - 1
        return (self.row, lax.rem(self.col + step, COLS))

    def beyond(self, way):
        step = 1 if way == 0 else BLOCKS - 1
        return (lax.rem(self.row + step, BLOCKS), self.col)

    def edge(self, side):
        return (pl.ds(160, 16), pl.ds(0, 16)) if side == 1 else (pl.ds(16, 16), pl.ds(176, 16))

    def copy(self, src, dst, send, recv, to):
        return pltpu.make_async_remote_copy(
            src_ref=src, dst_ref=dst, send_sem=send, recv_sem=recv, device_id=to, device_id_type=MESH
        )

    def strip(self, side):
        here, there = self.edge(side)
        rows = pl.ds(ROWS, ROWS)
        return self.copy(
            self.buf.at[rows, here, :], self.buf.at[rows, there, :], self.strip_sem.at[0, side], self.strip_sem.at[1, side],
            self.beside(side),
        )

    def block(self, way, j):
        src = pl.ds(ROWS + j * self.n, self.n)
        dst = pl.ds((0 if way == 0 else 2 * ROWS) + j * self.n, self.n)
        mid = pl.ds(16, 160)
        return self.copy(
            self.buf.at[src, mid, :], self.buf.at[dst, mid, :], self.row_sem.at[0, way, j], self.row_sem.at[1, way, j], self.beyond(way)
        )

    def relay(self, way, side, j):
        here, there = self.edge(side)
        rows = pl.ds((0 if way == 0 else 2 * ROWS) + j * self.n, self.n)
        return self.copy(
            self.buf.at[rows, here, :], self.buf.at[rows, there, :], self.relay_sem.at[0, way, side, j],
            self.relay_sem.at[1, way, side, j], self.beside(side),
        )

    def take(self, way, j):
        self.block(way, j).wait_recv()
        self.relay(way, 0, j).start()
        self.relay(way, 1, j).start()

    def took(self, way, j):
        self.relay(way, 0, j).wait_recv()
        self.relay(way, 1, j).wait_recv()

    def blank_columns(self, first, n):
        zeros = jnp.zeros((n, 16, self.buf.shape[2]), self.buf.dtype)

        @pl.when(self.col == 0)
        def _():
            self.buf[first : first + n, 0:16, :] = zeros

        @pl.when(self.col == COLS - 1)
        def _():
            self.buf[first : first + n, 176:192, :] = zeros

    def unfold(self, into, first, n, inside=None):
        c = self.buf.shape[2]
        self.blank_columns(first, n)

        def shift():
            def body(i, carry):
                r = first + i
                into[r, :, 0:c] = self.buf[r, 4:164, :]
                into[r, :, c : 2 * c] = self.buf[r, 16:176, :]
                into[r, :, 2 * c : 3 * c] = self.buf[r, 28:188, :]
                return carry

            lax.fori_loop(0, n, body, 0)

        if inside is None:
            shift()
            return
        pl.when(inside)(shift)

        @pl.when(jnp.logical_not(inside))
        def _():
            def body(i, carry):
                into[first + i] = jnp.zeros((160, 3 * c), into.dtype)
                return carry

            lax.fori_loop(0, n, body, 0)

    def drain(self):
        for side in range(2):
            self.strip(side).wait_send()
        for way in range(2):
            for j in range(self.chunks):
                self.block(way, j).wait_send()
                for side in range(2):
                    self.relay(way, side, j).wait_send()


def branch_kernel(scale, f_hbm, w_hbm, g_hbm, out, back, total, *scratch):
    (fx, gx, fim, gim, ft, w, w9, acc, partial, load_sem, f_strip, f_row, f_relay, g_strip, g_row, g_relay) = scratch[:16]
    where = position()
    row, col = where[0], where[1]
    mine = pl.ds(ROWS, ROWS)
    g_load = pltpu.make_async_copy(g_hbm, gx.at[mine, pl.ds(16, 160), :], load_sem.at[0])
    f_load = pltpu.make_async_copy(f_hbm, fx.at[mine, pl.ds(16, 160), :], load_sem.at[1])
    w_load = pltpu.make_async_copy(w_hbm, w, load_sem.at[2])
    g_load.start()
    f_load.start()
    w_load.start()
    f = Halo(fx, where, f_strip, f_row, f_relay, F_CHUNKS)
    g = Halo(gx, where, g_strip, g_row, g_relay, G_CHUNKS)
    red = [Reduction(k, where, partial, total, scratch[16:]) for k in range(3)]
    greet(where, (f.beside(0), f.beside(1), f.beyond(0), f.beyond(1)))

    g_load.wait()
    g.strip(0).start()
    g.strip(1).start()
    for j in range(G_CHUNKS):
        for way in range(2):
            g.block(way, j).start()
    f_load.wait()
    f.strip(0).start()
    f.strip(1).start()

    for i in range(3):
        ft[:, 640 * i : 640 * (i + 1)] = fx[ROWS + 4 * i : ROWS + 4 * (i + 1), 16:176, :].reshape(640, 256).T
    w_load.wait()
    for kb in range(3):
        for si in range(3):
            at = (3 * kb + si) * 128
            w9[:, at : at + 128] = w[2 - kb, 2 - si]

    above, below = row > 0, row < BLOCKS - 1

    def kernel_gradient(kb):
        pairs = gim[kb * ROWS : (kb + 1) * ROWS].reshape(ROWS * 160, 384)
        products = jnp.dot(ft[...], pairs, preferred_element_type=jnp.float32)
        for si in range(3):
            partial[2 - kb, (2 - si) * 256 : (3 - si) * 256, :] = products[:, si * 128 : (si + 1) * 128]
        red[2 - kb].to_core()

    def convolve(kb, first, n):
        piece = fim[kb * ROWS + first : kb * ROWS + first + n].reshape(n * 160, 768)
        return jnp.dot(piece, w[kb].reshape(768, 128), preferred_element_type=jnp.float32)

    def input_gradient(i):
        n = 4
        piece = jnp.concatenate(
            [gim[kb * ROWS + n * i : kb * ROWS + n * (i + 1)].reshape(n * 160, 384) for kb in range(3)], axis=1
        )
        grad = lax.dot_general(piece, w9[...], (((1,), (1,)), ((), ())), preferred_element_type=jnp.float32)
        back[n * i : n * (i + 1)] = grad.astype(back.dtype).reshape(n, 160, 256)

    g.strip(0).wait_recv()
    g.strip(1).wait_recv()
    g.unfold(gim, ROWS, ROWS)
    kernel_gradient(1)
    for j in range(F_CHUNKS):
        for way in range(2):
            f.block(way, j).start()

    f.strip(0).wait_recv()
    f.strip(1).wait_recv()
    f.unfold(fim, ROWS, ROWS)
    for i in range(3):
        acc[i * 640 : (i + 1) * 640, :] = convolve(1, 4 * i, 4)
    red[1].to_x()
    for j in range(G_CHUNKS):
        for way in range(2):
            g.take(way, j)
    red[1].to_z()
    for way, kb, inside in ((0, 0, above), (1, 2, below)):
        for j in range(G_CHUNKS):
            g.took(way, j)
        g.unfold(gim, kb * ROWS, ROWS, inside)
        kernel_gradient(kb)

    red[1].to_y()
    red[2].to_x()
    red[0].to_x()
    input_gradient(0)
    red[1].gather_z(scale)
    input_gradient(1)
    red[2].to_z()
    red[0].to_z()
    input_gradient(2)
    red[1].gather_x()
    red[2].to_y()
    red[0].to_y()
    red[1].gather_core()

    def features_taken(j):
        f.take(0, j)
        f.take(1, j)

    def features_used(j):
        n = ROWS // F_CHUNKS
        first = n * j
        f.took(0, j)
        f.took(1, j)
        f.unfold(fim, first, n, above)
        f.unfold(fim, 2 * ROWS + first, n, below)
        at = first * 160
        value = acc[at : at + n * 160, :] + convolve(0, first, n) + convolve(2, first, n)
        out[first : first + n] = value.astype(out.dtype).reshape(n, 160, 128)

    features_taken(0)
    features_taken(1)
    features_used(0)
    red[2].gather_z(scale)
    red[0].gather_z(scale)
    features_taken(2)
    features_used(1)
    red[2].gather_x()
    red[0].gather_x()
    features_taken(3)
    features_used(2)
    features_used(3)
    red[2].gather_core()
    red[0].gather_core()
    for k in (1, 2, 0):
        red[k].finish()
    for k in (1, 2, 0):
        red[k].drain()
    g.drain()
    f.drain()


def body(features, weight, cotangent):
    bf16, f32 = jnp.bfloat16, jnp.float32
    dma = pltpu.SemaphoreType.DMA
    pixels = ROWS * BLOCKS * 160 * COLS
    anywhere = pl.BlockSpec(memory_space=pl.ANY)
    vmem = pl.BlockSpec(memory_space=pltpu.VMEM)
    conv_out, input_grad, weight_grad = pl.pallas_call(
        functools.partial(branch_kernel, float(pixels) ** -0.5),
        out_shape=(
            jax.ShapeDtypeStruct((ROWS, 160, 128), bf16),
            jax.ShapeDtypeStruct((ROWS, 160, 256), bf16),
            jax.ShapeDtypeStruct((3, 768, 128), f32),
        ),
        in_specs=[anywhere] * 3,
        out_specs=(vmem, vmem, vmem),
        scratch_shapes=[
            pltpu.VMEM((3 * ROWS, 192, 256), bf16),
            pltpu.VMEM((3 * ROWS, 192, 128), bf16),
            pltpu.VMEM((3 * ROWS, 160, 768), bf16),
            pltpu.VMEM((3 * ROWS, 160, 384), bf16),
            pltpu.VMEM((256, ROWS * 160), bf16),
            pltpu.VMEM((3, 3, 256, 128), bf16),
            pltpu.VMEM((256, 1152), bf16),
            pltpu.VMEM((ROWS * 160, 128), f32),
            pltpu.VMEM((3, 768, 128), f32),
            dma((3,)),
            dma((2, 2)),
            dma((2, 2, F_CHUNKS)),
            dma((2, 2, 2, F_CHUNKS)),
            dma((2, 2)),
            dma((2, 2, G_CHUNKS)),
            dma((2, 2, 2, G_CHUNKS)),
        ]
        + reduction_scratch(3),
        compiler_params=pltpu.CompilerParams(collective_id=0, has_side_effects=True, vmem_limit_bytes=60 * 1024 * 1024),
        name="branch_kernel",
    )(features, weight, cotangent)
    return conv_out, input_grad, weight_grad.reshape(weight.shape)


def solution(mesh):
    placed = (P("rows", "cols", None), P(), P("rows", "cols", None))
    return jax.shard_map(
        body,
        mesh=mesh,
        in_specs=placed,
        out_specs=(P("rows", "cols", None), P("rows", "cols", None), P()),
        check_vma=False,
    )
```

```python
import functools

import jax
import jax.numpy as jnp
from jax import lax
from jax.experimental import pallas as pl
from jax.experimental.pallas import tpu as pltpu
from jax.sharding import PartitionSpec as P

ROWS = 12
BLOCKS, COLS = 32, 8
G_SIZES, F_SIZES = (4, 4, 4), (2, 3, 2, 2, 3)
G_DIRECT, F_DIRECT = 1, 0
VMEM_BYTES = 36 * 1024 * 1024
MESH = pl.DeviceIdType.MESH
NX, NY, NZ = 4, 4, 8
HALF, PART = 384, 16


def position():
    row, col = lax.axis_index("rows"), lax.axis_index("cols")
    return row, col, lax.div(col, 2), lax.rem(col, 2), lax.rem(row, NY), lax.div(row, NY)


def part_offset(i):
    return pl.multiple_of(lax.div(3 * i, 2) * 8, 8)


def rows_at(start, size):
    return pl.ds(pl.multiple_of(start, 8), size)


class Reduction:
    def __init__(self, piece, order, where, partial, total, scratch):
        self.k = piece
        self.row, self.col, self.x, self.core, self.y, self.z = where
        (self.half, self.s1, self.first, self.s2, self.second, self.ys, self.parts, self.near, self.first_sem, self.second_sem,
         self.ysem, self.parts_sem, self.whole_sem, self.far_sem) = scratch
        self.partial, self.total = partial, total
        self.order = order
        self.n1, self.n2 = (NX, NZ) if order == "xz" else (NZ, NX)
        self.i1, self.i2 = (self.x, self.z) if order == "xz" else (self.z, self.x)
        self.shard = HALF // self.n1

    def copy(self, src, dst, sems, slot, to):
        return pltpu.make_async_remote_copy(
            src_ref=src, dst_ref=dst, send_sem=sems.at[0, self.k, slot], recv_sem=sems.at[1, self.k, slot], device_id=to,
            device_id_type=MESH,
        )

    def partner(self):
        return (self.row, self.x * 2 + 1 - self.core)

    def along(self, axis, d):
        if axis == "x":
            return (self.row, lax.rem(self.x + d, NX) * 2 + self.core)
        if axis == "y":
            return (self.z * NY + lax.rem(self.y + d, NY), self.col)
        return (lax.rem(self.z + d, NZ) * NY + self.y, self.col)

    def core_copy(self):
        k = self.k
        return self.copy(self.partial.at[k, rows_at((1 - self.core) * HALF, HALF)], self.half.at[k], self.near, 0, self.partner())

    def first_copy(self, d):
        k = self.k
        target = lax.rem(self.i1 + d, self.n1)
        return self.copy(
            self.s1.at[k, rows_at(target * self.shard, self.shard)], self.first.at[k, d - 1, pl.ds(0, self.shard)], self.first_sem,
            d - 1, self.along(self.order[0], d),
        )

    def second_copy(self, d):
        k = self.k
        target = lax.rem(self.i2 + d, self.n2)
        return self.copy(
            self.s2.at[k, pl.ds(part_offset(target), PART)], self.second.at[k, d - 1], self.second_sem, d - 1,
            self.along(self.order[1], d),
        )

    def y_copy(self, d):
        return self.copy(self.ys.at[self.k, self.y], self.ys.at[self.k, self.y], self.ysem, d - 1, self.along("y", d))

    def part_copy(self, d):
        here = self.parts.at[self.k, self.i2]
        return self.copy(here, here, self.parts_sem, d - 1, self.along(self.order[1], d))

    def span(self, i):
        return self.total.at[self.k, rows_at(self.core * HALF + i * self.shard, self.shard)]

    def whole_copy(self, d):
        here = self.span(self.i1)
        return self.copy(here, here, self.whole_sem, d - 1, self.along(self.order[0], d))

    def far_copy(self, d):
        here = self.span(lax.rem(self.i1 + self.n1 - d, self.n1))
        return self.copy(here, here, self.far_sem, d, self.partner())

    def loop(self, n, body, start=1):
        if n <= 4:
            for d in range(start, n):
                body(d)
            return

        def step(d, carry):
            body(d)
            return carry

        lax.fori_loop(start, n, step, 0)

    def to_core(self):
        self.core_copy().start()

    def to_first(self):
        k = self.k
        self.core_copy().wait_recv()
        self.s1[k] = self.partial[k, rows_at(self.core * HALF, HALF)] + self.half[k]
        self.loop(self.n1, lambda d: self.first_copy(d).start())

    def to_second(self):
        k, n = self.k, self.shard
        self.loop(self.n1, lambda d: self.first_copy(d).wait_recv())
        value = self.s1[k, rows_at(self.i1 * n, n)]
        for d in range(self.n1 - 1):
            value = value + self.first[k, d, 0:n]
        self.s2[k, 0:n] = value
        self.loop(self.n2, lambda d: self.second_copy(d).start())

    def to_y(self):
        k = self.k
        self.loop(self.n2, lambda d: self.second_copy(d).wait_recv())
        mine = self.s2[k, pl.ds(part_offset(self.i2), PART)]
        for d in range(self.n2 - 1):
            mine = mine + self.second[k, d]
        self.ys[k, self.y] = mine
        for d in range(1, NY):
            self.y_copy(d).start()

    def gather_parts(self, scale):
        k = self.k
        for d in range(1, NY):
            self.y_copy(d).wait_recv()
        self.parts[k, self.i2] = (self.ys[k, 0] + self.ys[k, 1] + self.ys[k, 2] + self.ys[k, 3]) * scale
        self.loop(self.n2, lambda d: self.part_copy(d).start())

    def gather_whole(self):
        k = self.k
        self.loop(self.n2, lambda d: self.part_copy(d).wait_recv())
        base = self.core * HALF + self.i1 * self.shard
        for pair in range(self.n2 // 2):
            self.total[k, rows_at(base + 24 * pair, 16)] = self.parts[k, 2 * pair]
            self.total[k, rows_at(base + 24 * pair + 16, 8)] = self.parts[k, 2 * pair + 1, 8:16]
        self.loop(self.n1, lambda d: self.whole_copy(d).start())
        self.far_copy(0).start()

    def gather_core(self):
        def hand_on(d):
            self.whole_copy(d).wait_recv()
            self.far_copy(d).start()

        self.loop(self.n1, hand_on)

    def finish(self):
        self.loop(self.n1, lambda d: self.far_copy(d).wait_recv(), 0)

    def drain(self):
        self.core_copy().wait_send()
        self.loop(self.n1, lambda d: self.first_copy(d).wait_send())
        self.loop(self.n1, lambda d: self.whole_copy(d).wait_send())
        self.loop(self.n2, lambda d: self.second_copy(d).wait_send())
        self.loop(self.n2, lambda d: self.part_copy(d).wait_send())
        for d in range(1, NY):
            self.y_copy(d).wait_send()
        self.loop(self.n1, lambda d: self.far_copy(d).wait_send(), 0)


def reduction_scratch(pieces):
    f32 = jnp.float32
    dma = pltpu.SemaphoreType.DMA
    most = max(NX, NZ)
    return [
        pltpu.VMEM((pieces, HALF, 128), f32),
        pltpu.VMEM((pieces, HALF, 128), f32),
        pltpu.VMEM((pieces, most - 1, HALF // NX, 128), f32),
        pltpu.VMEM((pieces, HALF // NX, 128), f32),
        pltpu.VMEM((pieces, most - 1, PART, 128), f32),
        pltpu.VMEM((pieces, NY, PART, 128), f32),
        pltpu.VMEM((pieces, most, PART, 128), f32),
        dma((2, pieces, 1)),
        dma((2, pieces, most - 1)),
        dma((2, pieces, most - 1)),
        dma((2, pieces, NY - 1)),
        dma((2, pieces, most - 1)),
        dma((2, pieces, most - 1)),
        dma((2, pieces, most)),
    ]


def greet(where, extra=()):
    row, col, x, core, y, z = where
    barrier = pltpu.get_barrier_semaphore()

    def signal(to):
        pl.semaphore_signal(barrier, inc=1, device_id=to, device_id_type=MESH)

    count = 0
    for to in extra:
        signal(to)
        count += 1
    signal((row, x * 2 + 1 - core))
    for d in range(1, NX):
        signal((row, lax.rem(x + d, NX) * 2 + core))
    for d in range(1, NY):
        signal((z * NY + lax.rem(y + d, NY), col))

    def step(d, carry):
        signal((lax.rem(z + d, NZ) * NY + y, col))
        return carry

    lax.fori_loop(1, NZ, step, 0)
    pl.semaphore_wait(barrier, count + 1 + NX - 1 + NY - 1 + NZ - 1)


class Halo:
    def __init__(self, buf, where, strip_sem, row_sem, relay_sem, sizes, direct=0):
        self.buf = buf
        self.row, self.col = where[0], where[1]
        self.strip_sem, self.row_sem, self.relay_sem = strip_sem, row_sem, relay_sem
        self.sizes = sizes
        self.starts = [sum(sizes[:j]) for j in range(len(sizes))]
        self.chunks = len(sizes)
        self.relayed = self.chunks - direct

    def beside(self, side):
        step = 1 if side == 1 else COLS - 1
        return (self.row, lax.rem(self.col + step, COLS))

    def beyond(self, way):
        step = 1 if way == 0 else BLOCKS - 1
        return (lax.rem(self.row + step, BLOCKS), self.col)

    def edge(self, side):
        return (pl.ds(160, 16), pl.ds(0, 16)) if side == 1 else (pl.ds(16, 16), pl.ds(176, 16))

    def copy(self, src, dst, send, recv, to):
        return pltpu.make_async_remote_copy(
            src_ref=src, dst_ref=dst, send_sem=send, recv_sem=recv, device_id=to, device_id_type=MESH
        )

    def strip(self, side):
        here, there = self.edge(side)
        rows = pl.ds(ROWS, ROWS)
        return self.copy(
            self.buf.at[rows, here, :], self.buf.at[rows, there, :], self.strip_sem.at[0, side], self.strip_sem.at[1, side],
            self.beside(side),
        )

    def block(self, way, j):
        src = pl.ds(ROWS + self.starts[j], self.sizes[j])
        dst = pl.ds((0 if way == 0 else 2 * ROWS) + self.starts[j], self.sizes[j])
        mid = pl.ds(16, 160)
        return self.copy(
            self.buf.at[src, mid, :], self.buf.at[dst, mid, :], self.row_sem.at[0, way, j], self.row_sem.at[1, way, j], self.beyond(way)
        )

    def relay(self, way, side, j):
        here, there = self.edge(side)
        rows = pl.ds((0 if way == 0 else 2 * ROWS) + self.starts[j], self.sizes[j])
        source, to = rows, self.beside(side)
        if j >= self.relayed:
            source, to = pl.ds(ROWS + self.starts[j], self.sizes[j]), (self.beyond(way)[0], self.beside(side)[1])
        return self.copy(
            self.buf.at[source, here, :], self.buf.at[rows, there, :], self.relay_sem.at[0, way, side, j],
            self.relay_sem.at[1, way, side, j], to,
        )

    def send(self, j):
        if j >= self.relayed:
            for way in range(2):
                for side in range(2):
                    self.relay(way, side, j).start()
        for way in range(2):
            self.block(way, j).start()

    def corners(self):
        return [(self.beyond(way)[0], self.beside(side)[1]) for way in range(2) for side in range(2)]

    def take(self, way, j):
        self.block(way, j).wait_recv()
        if j < self.relayed:
            self.relay(way, 0, j).start()
            self.relay(way, 1, j).start()

    def took(self, way, j):
        self.relay(way, 0, j).wait_recv()
        self.relay(way, 1, j).wait_recv()

    def blank_columns(self, first, n):
        zeros = jnp.zeros((n, 16, self.buf.shape[2]), self.buf.dtype)

        @pl.when(self.col == 0)
        def _():
            self.buf[first : first + n, 0:16, :] = zeros

        @pl.when(self.col == COLS - 1)
        def _():
            self.buf[first : first + n, 176:192, :] = zeros

    def unfold(self, into, first, n, inside=None):
        c = self.buf.shape[2]
        self.blank_columns(first, n)

        def shift():
            def body(i, carry):
                r = first + i
                into[r, :, 0:c] = self.buf[r, 4:164, :]
                into[r, :, c : 2 * c] = self.buf[r, 16:176, :]
                into[r, :, 2 * c : 3 * c] = self.buf[r, 28:188, :]
                return carry

            lax.fori_loop(0, n, body, 0)

        if inside is None:
            shift()
            return
        pl.when(inside)(shift)

        @pl.when(jnp.logical_not(inside))
        def _():
            def body(i, carry):
                into[first + i] = jnp.zeros((160, 3 * c), into.dtype)
                return carry

            lax.fori_loop(0, n, body, 0)

    def drain(self):
        for side in range(2):
            self.strip(side).wait_send()
        for way in range(2):
            for j in range(self.chunks):
                self.block(way, j).wait_send()
                for side in range(2):
                    self.relay(way, side, j).wait_send()


def branch_kernel(scale, f_hbm, w_hbm, g_hbm, out, back, total, *scratch):
    (fx, gx, fim, gim, ft, w, w9, acc, partial, load_sem, f_strip, f_row, f_relay, g_strip, g_row, g_relay) = scratch[:16]
    where = position()
    row, col = where[0], where[1]
    mine = pl.ds(ROWS, ROWS)
    g_load = pltpu.make_async_copy(g_hbm, gx.at[mine, pl.ds(16, 160), :], load_sem.at[0])
    f_load = pltpu.make_async_copy(f_hbm, fx.at[mine, pl.ds(16, 160), :], load_sem.at[1])
    w_load = pltpu.make_async_copy(w_hbm, w, load_sem.at[2])
    g_load.start()
    f_load.start()
    w_load.start()
    f = Halo(fx, where, f_strip, f_row, f_relay, F_SIZES, F_DIRECT)
    g = Halo(gx, where, g_strip, g_row, g_relay, G_SIZES, G_DIRECT)
    red = [Reduction(k, order, where, partial, total, scratch[16:]) for k, order in enumerate(("xz", "xz", "xz"))]
    greet(where, (f.beside(0), f.beside(1), f.beyond(0), f.beyond(1), *(g.corners() if G_DIRECT + F_DIRECT else ())))

    g_load.wait()
    g.strip(0).start()
    g.strip(1).start()
    for j in range(len(G_SIZES)):
        g.send(j)
    f_load.wait()
    f.strip(0).start()
    f.strip(1).start()
    f.send(0)

    for i in range(3):
        ft[:, 640 * i : 640 * (i + 1)] = fx[ROWS + 4 * i : ROWS + 4 * (i + 1), 16:176, :].reshape(640, 256).T
    w_load.wait()
    for kb in range(3):
        for si in range(3):
            at = (3 * kb + si) * 128
            w9[:, at : at + 128] = w[2 - kb, 2 - si]

    above, below = row > 0, row < BLOCKS - 1

    def kernel_gradient(kb, i):
        pairs = gim[kb * ROWS + 4 * i : kb * ROWS + 4 * (i + 1)].reshape(640, 384)
        products = jnp.dot(ft[:, 640 * i : 640 * (i + 1)], pairs, preferred_element_type=jnp.float32)
        for si in range(3):
            tap = products[:, si * 128 : (si + 1) * 128]
            rows = slice((2 - si) * 256, (3 - si) * 256)
            partial[2 - kb, rows, :] = tap if i == 0 else partial[2 - kb, rows, :] + tap

    def convolve(kb, first, n):
        piece = fim[kb * ROWS + first : kb * ROWS + first + n].reshape(n * 160, 768)
        return jnp.dot(piece, w[kb].reshape(768, 128), preferred_element_type=jnp.float32)

    def input_gradient(i):
        n = 4
        piece = jnp.concatenate(
            [gim[kb * ROWS + n * i : kb * ROWS + n * (i + 1)].reshape(n * 160, 384) for kb in range(3)], axis=1
        )
        grad = lax.dot_general(piece, w9[...], (((1,), (1,)), ((), ())), preferred_element_type=jnp.float32)
        back[n * i : n * (i + 1)] = grad.astype(back.dtype).reshape(n, 160, 256)

    def features_taken(j):
        f.take(0, j)
        f.take(1, j)

    def features_used(j):
        n, first = f.sizes[j], f.starts[j]
        f.took(0, j)
        f.took(1, j)
        f.unfold(fim, first, n, above)
        f.unfold(fim, 2 * ROWS + first, n, below)
        at = first * 160
        value = acc[at : at + n * 160, :] + convolve(0, first, n) + convolve(2, first, n)
        out[first : first + n] = value.astype(out.dtype).reshape(n, 160, 128)

    def cotangent_used(i):
        for way, kb, inside in ((0, 0, above), (1, 2, below)):
            g.took(way, i)
            g.unfold(gim, kb * ROWS + 4 * i, 4, inside)
            kernel_gradient(kb, i)
            if i == len(G_SIZES) - 1:
                red[2 - kb].to_core()

    def cotangent_taken(i):
        g.take(0, i)
        g.take(1, i)

    g.strip(0).wait_recv()
    g.strip(1).wait_recv()
    g.unfold(gim, ROWS, ROWS)
    for i in range(3):
        kernel_gradient(1, i)
    red[1].to_core()
    f.strip(0).wait_recv()
    f.strip(1).wait_recv()
    f.unfold(fim, ROWS, ROWS)
    acc[0:640, :] = convolve(1, 0, 4)
    red[1].to_first()
    cotangent_taken(0)
    acc[640:1280, :] = convolve(1, 4, 4)
    acc[1280:1920, :] = convolve(1, 8, 4)
    cotangent_taken(1)
    cotangent_used(0)
    red[1].to_second()
    cotangent_used(1)
    cotangent_taken(2)
    cotangent_used(2)
    red[1].to_y()
    f.send(1)
    input_gradient(0)
    red[2].to_first()
    red[0].to_first()
    features_taken(0)
    red[1].gather_parts(scale)
    input_gradient(1)
    features_used(0)
    red[2].to_second()
    red[0].to_second()
    f.send(2)
    red[1].gather_whole()
    features_taken(1)
    input_gradient(2)
    features_used(1)
    red[2].to_y()
    red[0].to_y()
    f.send(3)
    features_taken(2)
    red[1].gather_core()
    features_used(2)
    red[2].gather_parts(scale)
    red[0].gather_parts(scale)
    f.send(4)
    features_taken(3)
    features_used(3)
    red[2].gather_whole()
    red[0].gather_whole()
    features_taken(4)
    red[2].gather_core()
    red[0].gather_core()
    features_used(4)
    for k in (1, 2, 0):
        red[k].finish()
    for k in (1, 2, 0):
        red[k].drain()
    g.drain()
    f.drain()


def body(features, weight, cotangent):
    bf16, f32 = jnp.bfloat16, jnp.float32
    dma = pltpu.SemaphoreType.DMA
    pixels = ROWS * BLOCKS * 160 * COLS
    anywhere = pl.BlockSpec(memory_space=pl.ANY)
    vmem = pl.BlockSpec(memory_space=pltpu.VMEM)
    conv_out, input_grad, weight_grad = pl.pallas_call(
        functools.partial(branch_kernel, float(pixels) ** -0.5),
        out_shape=(
            jax.ShapeDtypeStruct((ROWS, 160, 128), bf16),
            jax.ShapeDtypeStruct((ROWS, 160, 256), bf16),
            jax.ShapeDtypeStruct((3, 768, 128), f32),
        ),
        in_specs=[anywhere] * 3,
        out_specs=(vmem, vmem, vmem),
        scratch_shapes=[
            pltpu.VMEM((3 * ROWS, 192, 256), bf16),
            pltpu.VMEM((3 * ROWS, 192, 128), bf16),
            pltpu.VMEM((3 * ROWS, 160, 768), bf16),
            pltpu.VMEM((3 * ROWS, 160, 384), bf16),
            pltpu.VMEM((256, ROWS * 160), bf16),
            pltpu.VMEM((3, 3, 256, 128), bf16),
            pltpu.VMEM((256, 1152), bf16),
            pltpu.VMEM((ROWS * 160, 128), f32),
            pltpu.VMEM((3, 768, 128), f32),
            dma((3,)),
            dma((2, 2)),
            dma((2, 2, len(F_SIZES))),
            dma((2, 2, 2, len(F_SIZES))),
            dma((2, 2)),
            dma((2, 2, len(G_SIZES))),
            dma((2, 2, 2, len(G_SIZES))),
        ]
        + reduction_scratch(3),
        compiler_params=pltpu.CompilerParams(collective_id=0, has_side_effects=True, vmem_limit_bytes=VMEM_BYTES),
        name="branch_kernel",
    )(features, weight, cotangent)
    return conv_out, input_grad, weight_grad.reshape(weight.shape)


def solution(mesh):
    placed = (P("rows", "cols", None), P(), P("rows", "cols", None))
    return jax.shard_map(
        body,
        mesh=mesh,
        in_specs=placed,
        out_specs=(P("rows", "cols", None), P("rows", "cols", None), P()),
        check_vma=False,
    )
```

```python
import functools

import jax
import jax.numpy as jnp
from jax import lax
from jax.experimental import pallas as pl
from jax.experimental.pallas import tpu as pltpu
from jax.sharding import PartitionSpec as P

ROWS = 12
BLOCKS, COLS = 32, 8
G_SIZES, F_SIZES = (4, 4, 4), (2, 3, 2, 2, 3)
G_DIRECT, F_DIRECT = 1, 0
VMEM_BYTES = 36 * 1024 * 1024
MESH = pl.DeviceIdType.MESH
NX, NY, NZ = 4, 4, 8
HALF, PART = 384, 16


def position():
    row, col = lax.axis_index("rows"), lax.axis_index("cols")
    return row, col, lax.div(col, 2), lax.rem(col, 2), lax.rem(row, NY), lax.div(row, NY)


def part_offset(i):
    return pl.multiple_of(lax.div(3 * i, 2) * 8, 8)


def rows_at(start, size):
    return pl.ds(pl.multiple_of(start, 8), size)


class Reduction:
    def __init__(self, piece, order, where, partial, total, scratch):
        self.k = piece
        self.row, self.col, self.x, self.core, self.y, self.z = where
        (self.half, self.s1, self.first, self.s2, self.second, self.ys, self.parts, self.near, self.first_sem, self.second_sem,
         self.ysem, self.parts_sem, self.whole_sem, self.far_sem) = scratch
        self.partial, self.total = partial, total
        self.order = order
        self.n1, self.n2 = (NX, NZ) if order == "xz" else (NZ, NX)
        self.i1, self.i2 = (self.x, self.z) if order == "xz" else (self.z, self.x)
        self.shard = HALF // self.n1

    def copy(self, src, dst, sems, slot, to):
        return pltpu.make_async_remote_copy(
            src_ref=src, dst_ref=dst, send_sem=sems.at[0, self.k, slot], recv_sem=sems.at[1, self.k, slot], device_id=to,
            device_id_type=MESH,
        )

    def partner(self):
        return (self.row, self.x * 2 + 1 - self.core)

    def along(self, axis, d):
        if axis == "x":
            return (self.row, lax.rem(self.x + d, NX) * 2 + self.core)
        if axis == "y":
            return (self.z * NY + lax.rem(self.y + d, NY), self.col)
        return (lax.rem(self.z + d, NZ) * NY + self.y, self.col)

    def core_copy(self):
        k = self.k
        return self.copy(self.partial.at[k, rows_at((1 - self.core) * HALF, HALF)], self.half.at[k], self.near, 0, self.partner())

    def first_copy(self, d):
        k = self.k
        target = lax.rem(self.i1 + d, self.n1)
        return self.copy(
            self.s1.at[k, rows_at(target * self.shard, self.shard)], self.first.at[k, d - 1, pl.ds(0, self.shard)], self.first_sem,
            d - 1, self.along(self.order[0], d),
        )

    def second_copy(self, d):
        k = self.k
        target = lax.rem(self.i2 + d, self.n2)
        return self.copy(
            self.s2.at[k, pl.ds(part_offset(target), PART)], self.second.at[k, d - 1], self.second_sem, d - 1,
            self.along(self.order[1], d),
        )

    def y_copy(self, d):
        return self.copy(self.ys.at[self.k, self.y], self.ys.at[self.k, self.y], self.ysem, d - 1, self.along("y", d))

    def part_copy(self, d):
        here = self.parts.at[self.k, self.i2]
        return self.copy(here, here, self.parts_sem, d - 1, self.along(self.order[1], d))

    def span(self, i):
        return self.total.at[self.k, rows_at(self.core * HALF + i * self.shard, self.shard)]

    def whole_copy(self, d):
        here = self.span(self.i1)
        return self.copy(here, here, self.whole_sem, d - 1, self.along(self.order[0], d))

    def far_copy(self, d):
        here = self.span(lax.rem(self.i1 + self.n1 - d, self.n1))
        return self.copy(here, here, self.far_sem, d, self.partner())

    def loop(self, n, body, start=1):
        if n <= 4:
            for d in range(start, n):
                body(d)
            return

        def step(d, carry):
            body(d)
            return carry

        lax.fori_loop(start, n, step, 0)

    def to_core(self):
        self.core_copy().start()

    def to_first(self):
        k = self.k
        self.core_copy().wait_recv()
        self.s1[k] = self.partial[k, rows_at(self.core * HALF, HALF)] + self.half[k]
        self.loop(self.n1, lambda d: self.first_copy(d).start())

    def to_second(self):
        k, n = self.k, self.shard
        self.loop(self.n1, lambda d: self.first_copy(d).wait_recv())
        value = self.s1[k, rows_at(self.i1 * n, n)]
        for d in range(self.n1 - 1):
            value = value + self.first[k, d, 0:n]
        self.s2[k, 0:n] = value
        self.loop(self.n2, lambda d: self.second_copy(d).start())

    def to_y(self):
        k = self.k
        self.loop(self.n2, lambda d: self.second_copy(d).wait_recv())
        mine = self.s2[k, pl.ds(part_offset(self.i2), PART)]
        for d in range(self.n2 - 1):
            mine = mine + self.second[k, d]
        self.ys[k, self.y] = mine
        for d in range(1, NY):
            self.y_copy(d).start()

    def gather_parts(self, scale):
        k = self.k
        for d in range(1, NY):
            self.y_copy(d).wait_recv()
        self.parts[k, self.i2] = (self.ys[k, 0] + self.ys[k, 1] + self.ys[k, 2] + self.ys[k, 3]) * scale
        self.loop(self.n2, lambda d: self.part_copy(d).start())

    def gather_whole(self):
        k = self.k
        self.loop(self.n2, lambda d: self.part_copy(d).wait_recv())
        base = self.core * HALF + self.i1 * self.shard
        for pair in range(self.n2 // 2):
            self.total[k, rows_at(base + 24 * pair, 16)] = self.parts[k, 2 * pair]
            self.total[k, rows_at(base + 24 * pair + 16, 8)] = self.parts[k, 2 * pair + 1, 8:16]
        self.loop(self.n1, lambda d: self.whole_copy(d).start())
        self.far_copy(0).start()

    def gather_core(self):
        def hand_on(d):
            self.whole_copy(d).wait_recv()
            self.far_copy(d).start()

        self.loop(self.n1, hand_on)

    def finish(self):
        self.loop(self.n1, lambda d: self.far_copy(d).wait_recv(), 0)

    def drain(self):
        self.core_copy().wait_send()
        self.loop(self.n1, lambda d: self.first_copy(d).wait_send())
        self.loop(self.n1, lambda d: self.whole_copy(d).wait_send())
        self.loop(self.n2, lambda d: self.second_copy(d).wait_send())
        self.loop(self.n2, lambda d: self.part_copy(d).wait_send())
        for d in range(1, NY):
            self.y_copy(d).wait_send()
        self.loop(self.n1, lambda d: self.far_copy(d).wait_send(), 0)


def reduction_scratch(pieces):
    f32 = jnp.float32
    dma = pltpu.SemaphoreType.DMA
    most = max(NX, NZ)
    return [
        pltpu.VMEM((pieces, HALF, 128), f32),
        pltpu.VMEM((pieces, HALF, 128), f32),
        pltpu.VMEM((pieces, most - 1, HALF // NX, 128), f32),
        pltpu.VMEM((pieces, HALF // NX, 128), f32),
        pltpu.VMEM((pieces, most - 1, PART, 128), f32),
        pltpu.VMEM((pieces, NY, PART, 128), f32),
        pltpu.VMEM((pieces, most, PART, 128), f32),
        dma((2, pieces, 1)),
        dma((2, pieces, most - 1)),
        dma((2, pieces, most - 1)),
        dma((2, pieces, NY - 1)),
        dma((2, pieces, most - 1)),
        dma((2, pieces, most - 1)),
        dma((2, pieces, most)),
    ]


def greet(where, extra=()):
    row, col, x, core, y, z = where
    barrier = pltpu.get_barrier_semaphore()

    def signal(to):
        pl.semaphore_signal(barrier, inc=1, device_id=to, device_id_type=MESH)

    count = 0
    for to in extra:
        signal(to)
        count += 1
    signal((row, x * 2 + 1 - core))
    for d in range(1, NX):
        signal((row, lax.rem(x + d, NX) * 2 + core))
    for d in range(1, NY):
        signal((z * NY + lax.rem(y + d, NY), col))

    def step(d, carry):
        signal((lax.rem(z + d, NZ) * NY + y, col))
        return carry

    lax.fori_loop(1, NZ, step, 0)
    pl.semaphore_wait(barrier, count + 1 + NX - 1 + NY - 1 + NZ - 1)


class Halo:
    def __init__(self, buf, where, strip_sem, row_sem, relay_sem, sizes, direct=0):
        self.buf = buf
        self.row, self.col = where[0], where[1]
        self.strip_sem, self.row_sem, self.relay_sem = strip_sem, row_sem, relay_sem
        self.sizes = sizes
        self.starts = [sum(sizes[:j]) for j in range(len(sizes))]
        self.chunks = len(sizes)
        self.relayed = self.chunks - direct

    def beside(self, side):
        step = 1 if side == 1 else COLS - 1
        return (self.row, lax.rem(self.col + step, COLS))

    def beyond(self, way):
        step = 1 if way == 0 else BLOCKS - 1
        return (lax.rem(self.row + step, BLOCKS), self.col)

    def edge(self, side):
        return (pl.ds(160, 16), pl.ds(0, 16)) if side == 1 else (pl.ds(16, 16), pl.ds(176, 16))

    def copy(self, src, dst, send, recv, to):
        return pltpu.make_async_remote_copy(
            src_ref=src, dst_ref=dst, send_sem=send, recv_sem=recv, device_id=to, device_id_type=MESH
        )

    def strip(self, side):
        here, there = self.edge(side)
        rows = pl.ds(ROWS, ROWS)
        return self.copy(
            self.buf.at[rows, here, :], self.buf.at[rows, there, :], self.strip_sem.at[0, side], self.strip_sem.at[1, side],
            self.beside(side),
        )

    def block(self, way, j):
        src = pl.ds(ROWS + self.starts[j], self.sizes[j])
        dst = pl.ds((0 if way == 0 else 2 * ROWS) + self.starts[j], self.sizes[j])
        mid = pl.ds(16, 160)
        return self.copy(
            self.buf.at[src, mid, :], self.buf.at[dst, mid, :], self.row_sem.at[0, way, j], self.row_sem.at[1, way, j], self.beyond(way)
        )

    def relay(self, way, side, j):
        here, there = self.edge(side)
        rows = pl.ds((0 if way == 0 else 2 * ROWS) + self.starts[j], self.sizes[j])
        source, to = rows, self.beside(side)
        if j >= self.relayed:
            source, to = pl.ds(ROWS + self.starts[j], self.sizes[j]), (self.beyond(way)[0], self.beside(side)[1])
        return self.copy(
            self.buf.at[source, here, :], self.buf.at[rows, there, :], self.relay_sem.at[0, way, side, j],
            self.relay_sem.at[1, way, side, j], to,
        )

    def send(self, j):
        if j >= self.relayed:
            for way in range(2):
                for side in range(2):
                    self.relay(way, side, j).start()
        for way in range(2):
            self.block(way, j).start()

    def corners(self):
        return [(self.beyond(way)[0], self.beside(side)[1]) for way in range(2) for side in range(2)]

    def take(self, way, j):
        self.block(way, j).wait_recv()
        if j < self.relayed:
            self.relay(way, 0, j).start()
            self.relay(way, 1, j).start()

    def took(self, way, j):
        self.relay(way, 0, j).wait_recv()
        self.relay(way, 1, j).wait_recv()

    def blank_columns(self, first, n):
        zeros = jnp.zeros((n, 16, self.buf.shape[2]), self.buf.dtype)

        @pl.when(self.col == 0)
        def _():
            self.buf[first : first + n, 0:16, :] = zeros

        @pl.when(self.col == COLS - 1)
        def _():
            self.buf[first : first + n, 176:192, :] = zeros

    def unfold(self, into, first, n, inside=None):
        c = self.buf.shape[2]
        self.blank_columns(first, n)

        def shift():
            def body(i, carry):
                r = first + i
                into[r, :, 0:c] = self.buf[r, 4:164, :]
                into[r, :, c : 2 * c] = self.buf[r, 16:176, :]
                into[r, :, 2 * c : 3 * c] = self.buf[r, 28:188, :]
                return carry

            lax.fori_loop(0, n, body, 0)

        if inside is None:
            shift()
            return
        pl.when(inside)(shift)

        @pl.when(jnp.logical_not(inside))
        def _():
            def body(i, carry):
                into[first + i] = jnp.zeros((160, 3 * c), into.dtype)
                return carry

            lax.fori_loop(0, n, body, 0)

    def drain(self):
        for side in range(2):
            self.strip(side).wait_send()
        for way in range(2):
            for j in range(self.chunks):
                self.block(way, j).wait_send()
                for side in range(2):
                    self.relay(way, side, j).wait_send()


def branch_kernel(scale, f_hbm, w_hbm, g_hbm, out, back, total, *scratch):
    (fx, gx, fim, gim, ft, w, w9, acc, partial, load_sem, f_strip, f_row, f_relay, g_strip, g_row, g_relay) = scratch[:16]
    where = position()
    row, col = where[0], where[1]
    mine = pl.ds(ROWS, ROWS)
    g_load = pltpu.make_async_copy(g_hbm, gx.at[mine, pl.ds(16, 160), :], load_sem.at[0])
    f_load = pltpu.make_async_copy(f_hbm, fx.at[mine, pl.ds(16, 160), :], load_sem.at[1])
    w_load = pltpu.make_async_copy(w_hbm, w, load_sem.at[2])
    g_load.start()
    f_load.start()
    w_load.start()
    f = Halo(fx, where, f_strip, f_row, f_relay, F_SIZES, F_DIRECT)
    g = Halo(gx, where, g_strip, g_row, g_relay, G_SIZES, G_DIRECT)
    red = [Reduction(k, order, where, partial, total, scratch[16:]) for k, order in enumerate(("xz", "xz", "xz"))]
    greet(where, (f.beside(0), f.beside(1), f.beyond(0), f.beyond(1), *(g.corners() if G_DIRECT + F_DIRECT else ())))

    g_load.wait()
    g.strip(0).start()
    g.strip(1).start()
    for j in range(len(G_SIZES)):
        g.send(j)
    f_load.wait()
    f.strip(0).start()
    f.strip(1).start()
    f.send(0)

    for i in range(3):
        ft[:, 640 * i : 640 * (i + 1)] = fx[ROWS + 4 * i : ROWS + 4 * (i + 1), 16:176, :].reshape(640, 256).T
    w_load.wait()
    for kb in range(3):
        for si in range(3):
            at = (3 * kb + si) * 128
            w9[:, at : at + 128] = w[2 - kb, 2 - si]

    above, below = row > 0, row < BLOCKS - 1

    def kernel_gradient(kb, i):
        pairs = gim[kb * ROWS + 4 * i : kb * ROWS + 4 * (i + 1)].reshape(640, 384)
        products = jnp.dot(ft[:, 640 * i : 640 * (i + 1)], pairs, preferred_element_type=jnp.float32)
        for si in range(3):
            tap = products[:, si * 128 : (si + 1) * 128]
            rows = slice((2 - si) * 256, (3 - si) * 256)
            partial[2 - kb, rows, :] = tap if i == 0 else partial[2 - kb, rows, :] + tap

    def convolve(kb, first, n):
        piece = fim[kb * ROWS + first : kb * ROWS + first + n].reshape(n * 160, 768)
        return jnp.dot(piece, w[kb].reshape(768, 128), preferred_element_type=jnp.float32)

    def input_gradient(i):
        n = 4
        piece = jnp.concatenate(
            [gim[kb * ROWS + n * i : kb * ROWS + n * (i + 1)].reshape(n * 160, 384) for kb in range(3)], axis=1
        )
        grad = lax.dot_general(piece, w9[...], (((1,), (1,)), ((), ())), preferred_element_type=jnp.float32)
        back[n * i : n * (i + 1)] = grad.astype(back.dtype).reshape(n, 160, 256)

    def features_taken(j):
        f.take(0, j)
        f.take(1, j)

    def features_used(j):
        n, first = f.sizes[j], f.starts[j]
        f.took(0, j)
        f.took(1, j)
        f.unfold(fim, first, n, above)
        f.unfold(fim, 2 * ROWS + first, n, below)
        at = first * 160
        value = acc[at : at + n * 160, :] + convolve(0, first, n) + convolve(2, first, n)
        out[first : first + n] = value.astype(out.dtype).reshape(n, 160, 128)

    def cotangent_used(i):
        for way, kb, inside in ((0, 0, above), (1, 2, below)):
            g.took(way, i)
            g.unfold(gim, kb * ROWS + 4 * i, 4, inside)
            kernel_gradient(kb, i)
            if i == len(G_SIZES) - 1:
                red[2 - kb].to_core()

    def cotangent_taken(i):
        g.take(0, i)
        g.take(1, i)

    g.strip(0).wait_recv()
    g.strip(1).wait_recv()
    g.unfold(gim, ROWS, ROWS)
    for i in range(3):
        kernel_gradient(1, i)
    red[1].to_core()
    f.strip(0).wait_recv()
    f.strip(1).wait_recv()
    f.unfold(fim, ROWS, ROWS)
    acc[0:640, :] = convolve(1, 0, 4)
    red[1].to_first()
    cotangent_taken(0)
    acc[640:1280, :] = convolve(1, 4, 4)
    acc[1280:1920, :] = convolve(1, 8, 4)
    cotangent_taken(1)
    cotangent_used(0)
    red[1].to_second()
    cotangent_used(1)
    cotangent_taken(2)
    cotangent_used(2)
    red[1].to_y()
    f.send(1)
    input_gradient(0)
    red[2].to_first()
    red[0].to_first()
    features_taken(0)
    red[1].gather_parts(scale)
    input_gradient(1)
    features_used(0)
    red[2].to_second()
    red[0].to_second()
    f.send(2)
    red[1].gather_whole()
    features_taken(1)
    input_gradient(2)
    features_used(1)
    red[2].to_y()
    red[0].to_y()
    f.send(3)
    features_taken(2)
    red[1].gather_core()
    features_used(2)
    red[2].gather_parts(scale)
    red[0].gather_parts(scale)
    f.send(4)
    features_taken(3)
    features_used(3)
    red[2].gather_whole()
    red[0].gather_whole()
    features_taken(4)
    red[2].gather_core()
    red[0].gather_core()
    features_used(4)
    for k in (1, 2, 0):
        red[k].finish()
    for k in (1, 2, 0):
        red[k].drain()
    g.drain()
    f.drain()


def store_kernel(a, b, c, a_out, b_out, c_out, sem):
    copies = [pltpu.make_async_copy(src, dst, sem.at[i]) for i, (src, dst) in enumerate(((c, c_out), (b, b_out), (a, a_out)))]
    for copy in copies:
        copy.start()
    for copy in copies:
        copy.wait()


def stored(arrays):
    anywhere = pl.BlockSpec(memory_space=pl.ANY)
    return pl.pallas_call(
        store_kernel,
        out_shape=tuple(jax.ShapeDtypeStruct(x.shape, x.dtype) for x in arrays),
        in_specs=[anywhere] * 3,
        out_specs=(anywhere,) * 3,
        scratch_shapes=[pltpu.SemaphoreType.DMA((3,))],
        compiler_params=pltpu.CompilerParams(vmem_limit_bytes=1024 * 1024),
        name="store_kernel",
    )(*arrays)


def body(features, weight, cotangent):
    bf16, f32 = jnp.bfloat16, jnp.float32
    dma = pltpu.SemaphoreType.DMA
    pixels = ROWS * BLOCKS * 160 * COLS
    anywhere = pl.BlockSpec(memory_space=pl.ANY)
    vmem = pl.BlockSpec(memory_space=pltpu.VMEM)
    conv_out, input_grad, weight_grad = pl.pallas_call(
        functools.partial(branch_kernel, float(pixels) ** -0.5),
        out_shape=(
            jax.ShapeDtypeStruct((ROWS, 160, 128), bf16),
            jax.ShapeDtypeStruct((ROWS, 160, 256), bf16),
            jax.ShapeDtypeStruct((3, 768, 128), f32),
        ),
        in_specs=[anywhere] * 3,
        out_specs=(vmem, vmem, vmem),
        scratch_shapes=[
            pltpu.VMEM((3 * ROWS, 192, 256), bf16),
            pltpu.VMEM((3 * ROWS, 192, 128), bf16),
            pltpu.VMEM((3 * ROWS, 160, 768), bf16),
            pltpu.VMEM((3 * ROWS, 160, 384), bf16),
            pltpu.VMEM((256, ROWS * 160), bf16),
            pltpu.VMEM((3, 3, 256, 128), bf16),
            pltpu.VMEM((256, 1152), bf16),
            pltpu.VMEM((ROWS * 160, 128), f32),
            pltpu.VMEM((3, 768, 128), f32),
            dma((3,)),
            dma((2, 2)),
            dma((2, 2, len(F_SIZES))),
            dma((2, 2, 2, len(F_SIZES))),
            dma((2, 2)),
            dma((2, 2, len(G_SIZES))),
            dma((2, 2, 2, len(G_SIZES))),
        ]
        + reduction_scratch(3),
        compiler_params=pltpu.CompilerParams(collective_id=0, has_side_effects=True, vmem_limit_bytes=VMEM_BYTES),
        name="branch_kernel",
    )(*(pltpu.with_memory_space_constraint(x, pltpu.HBM) for x in (features, weight, cotangent)))
    conv_out, input_grad, weight_grad = stored((conv_out, input_grad, weight_grad))
    return conv_out, input_grad, weight_grad.reshape(weight.shape)


def solution(mesh):
    placed = (P("rows", "cols", None), P(), P("rows", "cols", None))
    return jax.shard_map(
        body,
        mesh=mesh,
        in_specs=placed,
        out_specs=(P("rows", "cols", None), P("rows", "cols", None), P()),
        check_vma=False,
    )
```

```python
import functools

import jax
import jax.numpy as jnp
from jax import lax
from jax.experimental import pallas as pl
from jax.experimental.pallas import tpu as pltpu
from jax.sharding import PartitionSpec as P

ROWS = 12
BLOCKS, COLS = 32, 8
G_SIZES, F_SIZES = (4, 4, 4), (2, 4, 1, 2, 3)
G_DIRECT, F_DIRECT = 1, 1
VMEM_BYTES = 36 * 1024 * 1024
MESH = pl.DeviceIdType.MESH
NX, NY, NZ = 4, 4, 8
HALF, PART = 384, 16


def position():
    row, col = lax.axis_index("rows"), lax.axis_index("cols")
    return row, col, lax.div(col, 2), lax.rem(col, 2), lax.rem(row, NY), lax.div(row, NY)


def part_offset(i):
    return pl.multiple_of(lax.div(3 * i, 2) * 8, 8)


def rows_at(start, size):
    return pl.ds(pl.multiple_of(start, 8), size)


class Reduction:
    def __init__(self, piece, order, where, partial, total, scratch):
        self.k = piece
        self.row, self.col, self.x, self.core, self.y, self.z = where
        (self.half, self.s1, self.first, self.s2, self.second, self.ys, self.near, self.first_sem, self.second_sem,
         self.ysem, self.parts_sem, self.whole_sem, self.far_sem) = scratch
        self.partial, self.total = partial, total
        self.order = order
        self.n1, self.n2 = (NX, NZ) if order == "xz" else (NZ, NX)
        self.i1, self.i2 = (self.x, self.z) if order == "xz" else (self.z, self.x)
        self.shard = HALF // self.n1

    def copy(self, src, dst, sems, slot, to):
        return pltpu.make_async_remote_copy(
            src_ref=src, dst_ref=dst, send_sem=sems.at[0, self.k, slot], recv_sem=sems.at[1, self.k, slot], device_id=to,
            device_id_type=MESH,
        )

    def partner(self):
        return (self.row, self.x * 2 + 1 - self.core)

    def along(self, axis, d):
        if axis == "x":
            return (self.row, lax.rem(self.x + d, NX) * 2 + self.core)
        if axis == "y":
            return (self.z * NY + lax.rem(self.y + d, NY), self.col)
        return (lax.rem(self.z + d, NZ) * NY + self.y, self.col)

    def core_copy(self):
        k = self.k
        return self.copy(self.partial.at[k, rows_at((1 - self.core) * HALF, HALF)], self.half.at[k], self.near, 0, self.partner())

    def first_copy(self, d):
        k = self.k
        target = lax.rem(self.i1 + d, self.n1)
        return self.copy(
            self.s1.at[k, rows_at(target * self.shard, self.shard)], self.first.at[k, d - 1, pl.ds(0, self.shard)], self.first_sem,
            d - 1, self.along(self.order[0], d),
        )

    def second_copy(self, d):
        k = self.k
        target = lax.rem(self.i2 + d, self.n2)
        return self.copy(
            self.s2.at[k, pl.ds(part_offset(target), PART)], self.second.at[k, d - 1], self.second_sem, d - 1,
            self.along(self.order[1], d),
        )

    def y_copy(self, d):
        return self.copy(self.ys.at[self.k, self.y], self.ys.at[self.k, self.y], self.ysem, d - 1, self.along("y", d))

    def parity(self, z, body):
        even = lax.rem(z, 2) == 0
        pl.when(even)(lambda: body(0, 16))
        pl.when(jnp.logical_not(even))(lambda: body(16, 8))

    def part_of(self, z, start, size):
        base = self.core * HALF + self.i1 * self.shard + lax.div(z, 2) * 24
        return self.total.at[self.k, rows_at(base + start, size)]

    def part_copies(self, d, act):
        def go(start, size):
            here = self.part_of(self.i2, start, size)
            act(self.copy(here, here, self.parts_sem, d - 1, self.along("z", d)))

        self.parity(self.i2, go)

    def take_part(self, d):
        source = lax.rem(self.i2 + NZ - d, NZ)

        def go(start, size):
            here = self.part_of(source, start, size)
            if not isinstance(d, int) or d:
                self.copy(here, here, self.parts_sem, d - 1, self.along("z", d)).wait_recv()
            for step in (2, 1, 3):
                self.copy(here, here, self.whole_sem, step - 1, self.along("x", step)).start()

        self.parity(source, go)

    def span(self, i):
        return self.total.at[self.k, rows_at(self.core * HALF + i * self.shard, self.shard)]

    def whole_copy(self, d):
        here = self.span(self.i1)
        return self.copy(here, here, self.whole_sem, d - 1, self.along(self.order[0], d))

    def far_copy(self, d):
        here = self.span(lax.rem(self.i1 + self.n1 - d, self.n1))
        return self.copy(here, here, self.far_sem, d, self.partner())

    def loop(self, n, body, start=1):
        if n <= 4:
            for d in range(start, n):
                body(d)
            return

        def step(d, carry):
            body(d)
            return carry

        lax.fori_loop(start, n, step, 0)

    def to_core(self):
        self.core_copy().start()

    def to_first(self):
        k = self.k
        self.core_copy().wait_recv()
        self.s1[k] = self.partial[k, rows_at(self.core * HALF, HALF)] + self.half[k]
        self.loop(self.n1, lambda d: self.first_copy(d).start())

    def to_second(self):
        k, n = self.k, self.shard
        self.loop(self.n1, lambda d: self.first_copy(d).wait_recv())
        value = self.s1[k, rows_at(self.i1 * n, n)]
        for d in range(self.n1 - 1):
            value = value + self.first[k, d, 0:n]
        self.s2[k, 0:n] = value
        self.loop(self.n2, lambda d: self.second_copy(d).start())

    def to_y(self):
        k = self.k
        self.loop(self.n2, lambda d: self.second_copy(d).wait_recv())
        mine = self.s2[k, pl.ds(part_offset(self.i2), PART)]
        for d in range(self.n2 - 1):
            mine = mine + self.second[k, d]
        self.ys[k, self.y] = mine
        for d in range(1, NY):
            self.y_copy(d).start()

    def gather_parts(self, scale):
        k = self.k
        for d in range(1, NY):
            self.y_copy(d).wait_recv()
        mine = (self.ys[k, 0] + self.ys[k, 1] + self.ys[k, 2] + self.ys[k, 3]) * scale
        base = self.core * HALF + self.i1 * self.shard + lax.div(self.i2, 2) * 24

        def keep(start, size):
            self.total[k, rows_at(base + start, size)] = mine[16 - size :]

        self.parity(self.i2, keep)
        self.loop(NZ, lambda d: self.part_copies(d, lambda copy: copy.start()))
        self.take_part(0)

    def gather_whole(self):
        for d in (1, 7, 2, 6, 3, 5, 4):
            self.take_part(d)
        self.far_copy(0).start()

    def gather_core(self):
        def hand_on(d):
            self.whole_copy(d).wait_recv()
            self.far_copy(d).start()

        self.loop(self.n1, hand_on)

    def finish(self):
        self.loop(self.n1, lambda d: self.far_copy(d).wait_recv(), 0)

    def drain(self):
        self.core_copy().wait_send()
        self.loop(self.n1, lambda d: self.first_copy(d).wait_send())
        self.loop(self.n1, lambda d: self.whole_copy(d).wait_send())
        self.loop(self.n2, lambda d: self.second_copy(d).wait_send())
        self.loop(NZ, lambda d: self.part_copies(d, lambda copy: copy.wait_send()))
        for d in range(1, NY):
            self.y_copy(d).wait_send()
        self.loop(self.n1, lambda d: self.far_copy(d).wait_send(), 0)


def reduction_scratch(pieces):
    f32 = jnp.float32
    dma = pltpu.SemaphoreType.DMA
    most = max(NX, NZ)
    return [
        pltpu.VMEM((pieces, HALF, 128), f32),
        pltpu.VMEM((pieces, HALF, 128), f32),
        pltpu.VMEM((pieces, most - 1, HALF // NX, 128), f32),
        pltpu.VMEM((pieces, HALF // NX, 128), f32),
        pltpu.VMEM((pieces, most - 1, PART, 128), f32),
        pltpu.VMEM((pieces, NY, PART, 128), f32),
        dma((2, pieces, 1)),
        dma((2, pieces, most - 1)),
        dma((2, pieces, most - 1)),
        dma((2, pieces, NY - 1)),
        dma((2, pieces, most - 1)),
        dma((2, pieces, most - 1)),
        dma((2, pieces, most)),
    ]


def greet(where, extra=()):
    row, col, x, core, y, z = where
    barrier = pltpu.get_barrier_semaphore()

    def signal(to):
        pl.semaphore_signal(barrier, inc=1, device_id=to, device_id_type=MESH)

    count = 0
    for to in extra:
        signal(to)
        count += 1
    signal((row, x * 2 + 1 - core))
    for d in range(1, NX):
        signal((row, lax.rem(x + d, NX) * 2 + core))
    for d in range(1, NY):
        signal((z * NY + lax.rem(y + d, NY), col))

    def step(d, carry):
        signal((lax.rem(z + d, NZ) * NY + y, col))
        return carry

    lax.fori_loop(1, NZ, step, 0)
    pl.semaphore_wait(barrier, count + 1 + NX - 1 + NY - 1 + NZ - 1)


class Halo:
    def __init__(self, buf, where, strip_sem, row_sem, relay_sem, sizes, direct=0):
        self.buf = buf
        self.row, self.col = where[0], where[1]
        self.strip_sem, self.row_sem, self.relay_sem = strip_sem, row_sem, relay_sem
        self.sizes = sizes
        self.starts = [sum(sizes[:j]) for j in range(len(sizes))]
        self.chunks = len(sizes)
        self.relayed = self.chunks - direct

    def beside(self, side):
        step = 1 if side == 1 else COLS - 1
        return (self.row, lax.rem(self.col + step, COLS))

    def beyond(self, way):
        step = 1 if way == 0 else BLOCKS - 1
        return (lax.rem(self.row + step, BLOCKS), self.col)

    def edge(self, side):
        return (pl.ds(160, 16), pl.ds(0, 16)) if side == 1 else (pl.ds(16, 16), pl.ds(176, 16))

    def copy(self, src, dst, send, recv, to):
        return pltpu.make_async_remote_copy(
            src_ref=src, dst_ref=dst, send_sem=send, recv_sem=recv, device_id=to, device_id_type=MESH
        )

    def strip(self, side):
        here, there = self.edge(side)
        rows = pl.ds(ROWS, ROWS)
        return self.copy(
            self.buf.at[rows, here, :], self.buf.at[rows, there, :], self.strip_sem.at[0, side], self.strip_sem.at[1, side],
            self.beside(side),
        )

    def block(self, way, j):
        src = pl.ds(ROWS + self.starts[j], self.sizes[j])
        dst = pl.ds((0 if way == 0 else 2 * ROWS) + self.starts[j], self.sizes[j])
        mid = pl.ds(16, 160)
        return self.copy(
            self.buf.at[src, mid, :], self.buf.at[dst, mid, :], self.row_sem.at[0, way, j], self.row_sem.at[1, way, j], self.beyond(way)
        )

    def relay(self, way, side, j):
        here, there = self.edge(side)
        rows = pl.ds((0 if way == 0 else 2 * ROWS) + self.starts[j], self.sizes[j])
        source, to = rows, self.beside(side)
        if j >= self.relayed:
            source, to = pl.ds(ROWS + self.starts[j], self.sizes[j]), (self.beyond(way)[0], self.beside(side)[1])
        return self.copy(
            self.buf.at[source, here, :], self.buf.at[rows, there, :], self.relay_sem.at[0, way, side, j],
            self.relay_sem.at[1, way, side, j], to,
        )

    def send(self, j):
        if j >= self.relayed:
            for way in range(2):
                for side in range(2):
                    self.relay(way, side, j).start()
        for way in range(2):
            self.block(way, j).start()

    def corners(self):
        return [(self.beyond(way)[0], self.beside(side)[1]) for way in range(2) for side in range(2)]

    def take(self, way, j):
        self.block(way, j).wait_recv()
        if j < self.relayed:
            self.relay(way, 0, j).start()
            self.relay(way, 1, j).start()

    def took(self, way, j):
        self.relay(way, 0, j).wait_recv()
        self.relay(way, 1, j).wait_recv()

    def blank_columns(self, first, n):
        zeros = jnp.zeros((n, 16, self.buf.shape[2]), self.buf.dtype)

        @pl.when(self.col == 0)
        def _():
            self.buf[first : first + n, 0:16, :] = zeros

        @pl.when(self.col == COLS - 1)
        def _():
            self.buf[first : first + n, 176:192, :] = zeros

    def unfold(self, into, first, n, inside=None):
        c = self.buf.shape[2]
        self.blank_columns(first, n)

        def shift():
            def body(i, carry):
                r = first + i
                into[r, :, 0:c] = self.buf[r, 4:164, :]
                into[r, :, c : 2 * c] = self.buf[r, 16:176, :]
                into[r, :, 2 * c : 3 * c] = self.buf[r, 28:188, :]
                return carry

            lax.fori_loop(0, n, body, 0)

        if inside is None:
            shift()
            return
        pl.when(inside)(shift)

        @pl.when(jnp.logical_not(inside))
        def _():
            def body(i, carry):
                into[first + i] = jnp.zeros((160, 3 * c), into.dtype)
                return carry

            lax.fori_loop(0, n, body, 0)

    def drain(self):
        for side in range(2):
            self.strip(side).wait_send()
        for way in range(2):
            for j in range(self.chunks):
                self.block(way, j).wait_send()
                for side in range(2):
                    self.relay(way, side, j).wait_send()


def branch_kernel(scale, f_hbm, w_hbm, g_hbm, out, back, total, *scratch):
    (fx, gx, fim, gim, ft, w, w9, acc, partial, load_sem, f_strip, f_row, f_relay, g_strip, g_row, g_relay) = scratch[:16]
    where = position()
    row, col = where[0], where[1]
    mine = pl.ds(ROWS, ROWS)
    g_load = pltpu.make_async_copy(g_hbm, gx.at[mine, pl.ds(16, 160), :], load_sem.at[0])
    f_load = pltpu.make_async_copy(f_hbm, fx.at[mine, pl.ds(16, 160), :], load_sem.at[1])
    w_load = pltpu.make_async_copy(w_hbm, w, load_sem.at[2])
    g_load.start()
    f_load.start()
    w_load.start()
    f = Halo(fx, where, f_strip, f_row, f_relay, F_SIZES, F_DIRECT)
    g = Halo(gx, where, g_strip, g_row, g_relay, G_SIZES, G_DIRECT)
    red = [Reduction(k, order, where, partial, total, scratch[16:]) for k, order in enumerate(("xz", "xz", "xz"))]
    greet(where, (f.beside(0), f.beside(1), f.beyond(0), f.beyond(1), *(g.corners() if G_DIRECT + F_DIRECT else ())))

    g_load.wait()
    g.strip(0).start()
    g.strip(1).start()
    for j in range(len(G_SIZES)):
        g.send(j)
    f_load.wait()
    f.strip(0).start()
    f.strip(1).start()
    f.send(0)

    for i in range(3):
        ft[:, 640 * i : 640 * (i + 1)] = fx[ROWS + 4 * i : ROWS + 4 * (i + 1), 16:176, :].reshape(640, 256).T
    w_load.wait()
    for kb in range(3):
        for si in range(3):
            at = (3 * kb + si) * 128
            w9[:, at : at + 128] = w[2 - kb, 2 - si]

    above, below = row > 0, row < BLOCKS - 1

    def kernel_gradient(kb, i):
        pairs = gim[kb * ROWS + 4 * i : kb * ROWS + 4 * (i + 1)].reshape(640, 384)
        products = jnp.dot(ft[:, 640 * i : 640 * (i + 1)], pairs, preferred_element_type=jnp.float32)
        for si in range(3):
            tap = products[:, si * 128 : (si + 1) * 128]
            rows = slice((2 - si) * 256, (3 - si) * 256)
            partial[2 - kb, rows, :] = tap if i == 0 else partial[2 - kb, rows, :] + tap

    def convolve(kb, first, n):
        piece = fim[kb * ROWS + first : kb * ROWS + first + n].reshape(n * 160, 768)
        return jnp.dot(piece, w[kb].reshape(768, 128), preferred_element_type=jnp.float32)

    def input_gradient(i):
        n = 4
        piece = jnp.concatenate(
            [gim[kb * ROWS + n * i : kb * ROWS + n * (i + 1)].reshape(n * 160, 384) for kb in range(3)], axis=1
        )
        grad = lax.dot_general(piece, w9[...], (((1,), (1,)), ((), ())), preferred_element_type=jnp.float32)
        back[n * i : n * (i + 1)] = grad.astype(back.dtype).reshape(n, 160, 256)

    def features_taken(j):
        f.take(0, j)
        f.take(1, j)

    def features_used(j):
        n, first = f.sizes[j], f.starts[j]
        f.took(0, j)
        f.took(1, j)
        f.unfold(fim, first, n, above)
        f.unfold(fim, 2 * ROWS + first, n, below)
        at = first * 160
        value = acc[at : at + n * 160, :] + convolve(0, first, n) + convolve(2, first, n)
        out[first : first + n] = value.astype(out.dtype).reshape(n, 160, 128)

    def cotangent_used(i):
        for way, kb, inside in ((0, 0, above), (1, 2, below)):
            g.took(way, i)
            g.unfold(gim, kb * ROWS + 4 * i, 4, inside)
            kernel_gradient(kb, i)
            if i == len(G_SIZES) - 1:
                red[2 - kb].to_core()

    def cotangent_taken(i):
        g.take(0, i)
        g.take(1, i)

    g.strip(0).wait_recv()
    g.strip(1).wait_recv()
    g.unfold(gim, ROWS, ROWS)
    for i in range(3):
        kernel_gradient(1, i)
    red[1].to_core()
    f.strip(0).wait_recv()
    f.strip(1).wait_recv()
    f.unfold(fim, ROWS, ROWS)
    acc[0:640, :] = convolve(1, 0, 4)
    red[1].to_first()
    cotangent_taken(0)
    acc[640:1280, :] = convolve(1, 4, 4)
    acc[1280:1920, :] = convolve(1, 8, 4)
    cotangent_taken(1)
    cotangent_used(0)
    red[1].to_second()
    cotangent_used(1)
    cotangent_taken(2)
    cotangent_used(2)
    red[1].to_y()
    f.send(1)
    input_gradient(0)
    red[2].to_first()
    red[0].to_first()
    features_taken(0)
    red[1].gather_parts(scale)
    input_gradient(1)
    features_used(0)
    red[2].to_second()
    red[0].to_second()
    f.send(2)
    red[1].gather_whole()
    features_taken(1)
    input_gradient(2)
    features_used(1)
    red[2].to_y()
    red[0].to_y()
    f.send(3)
    features_taken(2)
    red[1].gather_core()
    features_used(2)
    red[2].gather_parts(scale)
    red[0].gather_parts(scale)
    f.send(4)
    for d in (1, 7, 2, 6):
        red[2].take_part(d)
        red[0].take_part(d)
    features_taken(3)
    for d in (3, 5, 4):
        red[2].take_part(d)
        red[0].take_part(d)
    red[2].far_copy(0).start()
    red[0].far_copy(0).start()
    features_used(3)
    features_taken(4)
    red[2].gather_core()
    red[0].gather_core()
    features_used(4)
    for k in (1, 2, 0):
        red[k].finish()
    for k in (1, 2, 0):
        red[k].drain()
    g.drain()
    f.drain()


def store_kernel(a, b, c, a_out, b_out, c_out, sem):
    copies = [pltpu.make_async_copy(src, dst, sem.at[i]) for i, (src, dst) in enumerate(((c, c_out), (b, b_out), (a, a_out)))]
    for copy in copies:
        copy.start()
    for copy in copies:
        copy.wait()


def stored(arrays):
    anywhere = pl.BlockSpec(memory_space=pl.ANY)
    return pl.pallas_call(
        store_kernel,
        out_shape=tuple(jax.ShapeDtypeStruct(x.shape, x.dtype) for x in arrays),
        in_specs=[anywhere] * 3,
        out_specs=(anywhere,) * 3,
        scratch_shapes=[pltpu.SemaphoreType.DMA((3,))],
        compiler_params=pltpu.CompilerParams(vmem_limit_bytes=1024 * 1024),
        name="store_kernel",
    )(*arrays)


def body(features, weight, cotangent):
    bf16, f32 = jnp.bfloat16, jnp.float32
    dma = pltpu.SemaphoreType.DMA
    pixels = ROWS * BLOCKS * 160 * COLS
    anywhere = pl.BlockSpec(memory_space=pl.ANY)
    vmem = pl.BlockSpec(memory_space=pltpu.VMEM)
    conv_out, input_grad, weight_grad = pl.pallas_call(
        functools.partial(branch_kernel, float(pixels) ** -0.5),
        out_shape=(
            jax.ShapeDtypeStruct((ROWS, 160, 128), bf16),
            jax.ShapeDtypeStruct((ROWS, 160, 256), bf16),
            jax.ShapeDtypeStruct((3, 768, 128), f32),
        ),
        in_specs=[anywhere] * 3,
        out_specs=(vmem, vmem, vmem),
        scratch_shapes=[
            pltpu.VMEM((3 * ROWS, 192, 256), bf16),
            pltpu.VMEM((3 * ROWS, 192, 128), bf16),
            pltpu.VMEM((3 * ROWS, 160, 768), bf16),
            pltpu.VMEM((3 * ROWS, 160, 384), bf16),
            pltpu.VMEM((256, ROWS * 160), bf16),
            pltpu.VMEM((3, 3, 256, 128), bf16),
            pltpu.VMEM((256, 1152), bf16),
            pltpu.VMEM((ROWS * 160, 128), f32),
            pltpu.VMEM((3, 768, 128), f32),
            dma((3,)),
            dma((2, 2)),
            dma((2, 2, len(F_SIZES))),
            dma((2, 2, 2, len(F_SIZES))),
            dma((2, 2)),
            dma((2, 2, len(G_SIZES))),
            dma((2, 2, 2, len(G_SIZES))),
        ]
        + reduction_scratch(3),
        compiler_params=pltpu.CompilerParams(collective_id=0, has_side_effects=True, vmem_limit_bytes=VMEM_BYTES),
        name="branch_kernel",
    )(*(pltpu.with_memory_space_constraint(x, pltpu.HBM) for x in (features, weight, cotangent)))
    conv_out, input_grad, weight_grad = stored((conv_out, input_grad, weight_grad))
    return conv_out, input_grad, weight_grad.reshape(weight.shape)


def solution(mesh):
    placed = (P("rows", "cols", None), P(), P("rows", "cols", None))
    return jax.shard_map(
        body,
        mesh=mesh,
        in_specs=placed,
        out_specs=(P("rows", "cols", None), P("rows", "cols", None), P()),
        check_vma=False,
    )
```

```python
import functools

import jax
import jax.numpy as jnp
from jax import lax
from jax.experimental import pallas as pl
from jax.experimental.pallas import tpu as pltpu
from jax.sharding import PartitionSpec as P

ROWS = 12
BLOCKS, COLS = 32, 8
G_SIZES, F_SIZES = (4, 4, 4), (2, 4, 1, 2, 2, 1)
G_DIRECT, F_DIRECT = 1, 1
VMEM_BYTES = 36 * 1024 * 1024
MESH = pl.DeviceIdType.MESH
NX, NY, NZ = 4, 4, 8
HALF, PART = 384, 16


def position():
    row, col = lax.axis_index("rows"), lax.axis_index("cols")
    return row, col, lax.div(col, 2), lax.rem(col, 2), lax.rem(row, NY), lax.div(row, NY)


def part_offset(i):
    return pl.multiple_of(lax.div(3 * i, 2) * 8, 8)


def rows_at(start, size):
    return pl.ds(pl.multiple_of(start, 8), size)


class Reduction:
    def __init__(self, piece, order, where, partial, total, scratch):
        self.k = piece
        self.row, self.col, self.x, self.core, self.y, self.z = where
        (self.half, self.s1, self.first, self.s2, self.second, self.ys, self.near, self.first_sem, self.second_sem,
         self.ysem, self.parts_sem, self.whole_sem, self.far_sem) = scratch
        self.partial, self.total = partial, total
        self.order = order
        self.n1, self.n2 = (NX, NZ) if order == "xz" else (NZ, NX)
        self.i1, self.i2 = (self.x, self.z) if order == "xz" else (self.z, self.x)
        self.shard = HALF // self.n1

    def copy(self, src, dst, sems, slot, to):
        return pltpu.make_async_remote_copy(
            src_ref=src, dst_ref=dst, send_sem=sems.at[0, self.k, slot], recv_sem=sems.at[1, self.k, slot], device_id=to,
            device_id_type=MESH,
        )

    def partner(self):
        return (self.row, self.x * 2 + 1 - self.core)

    def along(self, axis, d):
        if axis == "x":
            return (self.row, lax.rem(self.x + d, NX) * 2 + self.core)
        if axis == "y":
            return (self.z * NY + lax.rem(self.y + d, NY), self.col)
        return (lax.rem(self.z + d, NZ) * NY + self.y, self.col)

    def core_copy(self):
        k = self.k
        return self.copy(self.partial.at[k, rows_at((1 - self.core) * HALF, HALF)], self.half.at[k], self.near, 0, self.partner())

    def first_copy(self, d):
        k = self.k
        target = lax.rem(self.i1 + d, self.n1)
        return self.copy(
            self.s1.at[k, rows_at(target * self.shard, self.shard)], self.first.at[k, d - 1, pl.ds(0, self.shard)], self.first_sem,
            d - 1, self.along(self.order[0], d),
        )

    def second_copy(self, d):
        k = self.k
        target = lax.rem(self.i2 + d, self.n2)
        return self.copy(
            self.s2.at[k, pl.ds(part_offset(target), PART)], self.second.at[k, d - 1], self.second_sem, d - 1,
            self.along(self.order[1], d),
        )

    def y_copy(self, d):
        return self.copy(self.ys.at[self.k, self.y], self.ys.at[self.k, self.y], self.ysem, d - 1, self.along("y", d))

    def parity(self, z, body):
        even = lax.rem(z, 2) == 0
        pl.when(even)(lambda: body(0, 16))
        pl.when(jnp.logical_not(even))(lambda: body(16, 8))

    def part_of(self, z, start, size):
        base = self.core * HALF + self.i1 * self.shard + lax.div(z, 2) * 24
        return self.total.at[self.k, rows_at(base + start, size)]

    def part_copies(self, d, act):
        def go(start, size):
            here = self.part_of(self.i2, start, size)
            act(self.copy(here, here, self.parts_sem, d - 1, self.along("z", d)))

        self.parity(self.i2, go)

    def take_part(self, d):
        source = lax.rem(self.i2 + NZ - d, NZ)

        def go(start, size):
            here = self.part_of(source, start, size)
            if not isinstance(d, int) or d:
                self.copy(here, here, self.parts_sem, d - 1, self.along("z", d)).wait_recv()
            for step in (1, 3, 2):
                self.copy(here, here, self.whole_sem, step - 1, self.along("x", step)).start()

        self.parity(source, go)

    def span(self, i):
        return self.total.at[self.k, rows_at(self.core * HALF + i * self.shard, self.shard)]

    def whole_copy(self, d):
        here = self.span(self.i1)
        return self.copy(here, here, self.whole_sem, d - 1, self.along(self.order[0], d))

    def far_copy(self, d):
        here = self.span(lax.rem(self.i1 + self.n1 - d, self.n1))
        return self.copy(here, here, self.far_sem, d, self.partner())

    def loop(self, n, body, start=1):
        if n <= 4:
            for d in range(start, n):
                body(d)
            return

        def step(d, carry):
            body(d)
            return carry

        lax.fori_loop(start, n, step, 0)

    def to_core(self):
        self.core_copy().start()

    def to_first(self):
        k = self.k
        self.core_copy().wait_recv()
        self.s1[k] = self.partial[k, rows_at(self.core * HALF, HALF)] + self.half[k]
        self.loop(self.n1, lambda d: self.first_copy(d).start())

    def to_second(self):
        k, n = self.k, self.shard
        self.loop(self.n1, lambda d: self.first_copy(d).wait_recv())
        value = self.s1[k, rows_at(self.i1 * n, n)]
        for d in range(self.n1 - 1):
            value = value + self.first[k, d, 0:n]
        self.s2[k, 0:n] = value
        self.loop(self.n2, lambda d: self.second_copy(d).start())

    def to_y(self):
        k = self.k
        self.loop(self.n2, lambda d: self.second_copy(d).wait_recv())
        mine = self.s2[k, pl.ds(part_offset(self.i2), PART)]
        for d in range(self.n2 - 1):
            mine = mine + self.second[k, d]
        self.ys[k, self.y] = mine
        for d in range(1, NY):
            self.y_copy(d).start()

    def gather_parts(self, scale):
        k = self.k
        for d in range(1, NY):
            self.y_copy(d).wait_recv()
        mine = (self.ys[k, 0] + self.ys[k, 1] + self.ys[k, 2] + self.ys[k, 3]) * scale
        base = self.core * HALF + self.i1 * self.shard + lax.div(self.i2, 2) * 24

        def keep(start, size):
            self.total[k, rows_at(base + start, size)] = mine[16 - size :]

        self.parity(self.i2, keep)
        self.loop(NZ, lambda d: self.part_copies(d, lambda copy: copy.start()))
        self.take_part(0)

    def gather_whole(self):
        for d in (1, 7, 2, 6, 3, 5, 4):
            self.take_part(d)
        self.far_copy(0).start()

    def gather_core(self):
        def hand_on(d):
            self.whole_copy(d).wait_recv()
            self.far_copy(d).start()

        self.loop(self.n1, hand_on)

    def finish(self):
        self.loop(self.n1, lambda d: self.far_copy(d).wait_recv(), 0)

    def drain(self):
        self.core_copy().wait_send()
        self.loop(self.n1, lambda d: self.first_copy(d).wait_send())
        self.loop(self.n1, lambda d: self.whole_copy(d).wait_send())
        self.loop(self.n2, lambda d: self.second_copy(d).wait_send())
        self.loop(NZ, lambda d: self.part_copies(d, lambda copy: copy.wait_send()))
        for d in range(1, NY):
            self.y_copy(d).wait_send()
        self.loop(self.n1, lambda d: self.far_copy(d).wait_send(), 0)


def reduction_scratch(pieces):
    f32 = jnp.float32
    dma = pltpu.SemaphoreType.DMA
    most = max(NX, NZ)
    return [
        pltpu.VMEM((pieces, HALF, 128), f32),
        pltpu.VMEM((pieces, HALF, 128), f32),
        pltpu.VMEM((pieces, most - 1, HALF // NX, 128), f32),
        pltpu.VMEM((pieces, HALF // NX, 128), f32),
        pltpu.VMEM((pieces, most - 1, PART, 128), f32),
        pltpu.VMEM((pieces, NY, PART, 128), f32),
        dma((2, pieces, 1)),
        dma((2, pieces, most - 1)),
        dma((2, pieces, most - 1)),
        dma((2, pieces, NY - 1)),
        dma((2, pieces, most - 1)),
        dma((2, pieces, most - 1)),
        dma((2, pieces, most)),
    ]


def greet(where, extra=()):
    row, col, x, core, y, z = where
    barrier = pltpu.get_barrier_semaphore()

    def signal(to):
        pl.semaphore_signal(barrier, inc=1, device_id=to, device_id_type=MESH)

    count = 0
    for to in extra:
        signal(to)
        count += 1
    signal((row, x * 2 + 1 - core))
    for d in range(1, NX):
        signal((row, lax.rem(x + d, NX) * 2 + core))
    for d in range(1, NY):
        signal((z * NY + lax.rem(y + d, NY), col))

    def step(d, carry):
        signal((lax.rem(z + d, NZ) * NY + y, col))
        return carry

    lax.fori_loop(1, NZ, step, 0)
    pl.semaphore_wait(barrier, count + 1 + NX - 1 + NY - 1 + NZ - 1)


class Halo:
    def __init__(self, buf, where, strip_sem, row_sem, relay_sem, sizes, direct=0):
        self.buf = buf
        self.row, self.col = where[0], where[1]
        self.strip_sem, self.row_sem, self.relay_sem = strip_sem, row_sem, relay_sem
        self.sizes = sizes
        self.starts = [sum(sizes[:j]) for j in range(len(sizes))]
        self.chunks = len(sizes)
        self.relayed = self.chunks - direct

    def beside(self, side):
        step = 1 if side == 1 else COLS - 1
        return (self.row, lax.rem(self.col + step, COLS))

    def beyond(self, way):
        step = 1 if way == 0 else BLOCKS - 1
        return (lax.rem(self.row + step, BLOCKS), self.col)

    def edge(self, side):
        return (pl.ds(160, 16), pl.ds(0, 16)) if side == 1 else (pl.ds(16, 16), pl.ds(176, 16))

    def copy(self, src, dst, send, recv, to):
        return pltpu.make_async_remote_copy(
            src_ref=src, dst_ref=dst, send_sem=send, recv_sem=recv, device_id=to, device_id_type=MESH
        )

    def strip(self, side):
        here, there = self.edge(side)
        rows = pl.ds(ROWS, ROWS)
        return self.copy(
            self.buf.at[rows, here, :], self.buf.at[rows, there, :], self.strip_sem.at[0, side], self.strip_sem.at[1, side],
            self.beside(side),
        )

    def block(self, way, j):
        src = pl.ds(ROWS + self.starts[j], self.sizes[j])
        dst = pl.ds((0 if way == 0 else 2 * ROWS) + self.starts[j], self.sizes[j])
        mid = pl.ds(16, 160)
        return self.copy(
            self.buf.at[src, mid, :], self.buf.at[dst, mid, :], self.row_sem.at[0, way, j], self.row_sem.at[1, way, j], self.beyond(way)
        )

    def relay(self, way, side, j):
        here, there = self.edge(side)
        rows = pl.ds((0 if way == 0 else 2 * ROWS) + self.starts[j], self.sizes[j])
        source, to = rows, self.beside(side)
        if j >= self.relayed:
            source, to = pl.ds(ROWS + self.starts[j], self.sizes[j]), (self.beyond(way)[0], self.beside(side)[1])
        return self.copy(
            self.buf.at[source, here, :], self.buf.at[rows, there, :], self.relay_sem.at[0, way, side, j],
            self.relay_sem.at[1, way, side, j], to,
        )

    def send(self, j):
        if j >= self.relayed:
            for way in range(2):
                for side in range(2):
                    self.relay(way, side, j).start()
        for way in range(2):
            self.block(way, j).start()

    def corners(self):
        return [(self.beyond(way)[0], self.beside(side)[1]) for way in range(2) for side in range(2)]

    def take(self, way, j):
        self.block(way, j).wait_recv()
        if j < self.relayed:
            self.relay(way, 0, j).start()
            self.relay(way, 1, j).start()

    def took(self, way, j):
        self.relay(way, 0, j).wait_recv()
        self.relay(way, 1, j).wait_recv()

    def blank_columns(self, first, n):
        zeros = jnp.zeros((n, 16, self.buf.shape[2]), self.buf.dtype)

        @pl.when(self.col == 0)
        def _():
            self.buf[first : first + n, 0:16, :] = zeros

        @pl.when(self.col == COLS - 1)
        def _():
            self.buf[first : first + n, 176:192, :] = zeros

    def unfold(self, into, first, n, inside=None):
        c = self.buf.shape[2]
        self.blank_columns(first, n)

        def shift():
            def body(i, carry):
                r = first + i
                into[r, :, 0:c] = self.buf[r, 4:164, :]
                into[r, :, c : 2 * c] = self.buf[r, 16:176, :]
                into[r, :, 2 * c : 3 * c] = self.buf[r, 28:188, :]
                return carry

            lax.fori_loop(0, n, body, 0)

        if inside is None:
            shift()
            return
        pl.when(inside)(shift)

        @pl.when(jnp.logical_not(inside))
        def _():
            def body(i, carry):
                into[first + i] = jnp.zeros((160, 3 * c), into.dtype)
                return carry

            lax.fori_loop(0, n, body, 0)

    def drain(self):
        for side in range(2):
            self.strip(side).wait_send()
        for way in range(2):
            for j in range(self.chunks):
                self.block(way, j).wait_send()
                for side in range(2):
                    self.relay(way, side, j).wait_send()


def branch_kernel(scale, f_hbm, w_hbm, g_hbm, out, back, total, *scratch):
    (fx, gx, fim, gim, ft, w, w9, acc, partial, load_sem, f_strip, f_row, f_relay, g_strip, g_row, g_relay) = scratch[:16]
    where = position()
    row, col = where[0], where[1]
    mine = pl.ds(ROWS, ROWS)
    g_load = pltpu.make_async_copy(g_hbm, gx.at[mine, pl.ds(16, 160), :], load_sem.at[0])
    f_load = pltpu.make_async_copy(f_hbm, fx.at[mine, pl.ds(16, 160), :], load_sem.at[1])
    w_load = pltpu.make_async_copy(w_hbm, w, load_sem.at[2])
    g_load.start()
    f_load.start()
    w_load.start()
    f = Halo(fx, where, f_strip, f_row, f_relay, F_SIZES, F_DIRECT)
    g = Halo(gx, where, g_strip, g_row, g_relay, G_SIZES, G_DIRECT)
    red = [Reduction(k, order, where, partial, total, scratch[16:]) for k, order in enumerate(("xz", "xz", "xz"))]
    greet(where, (f.beside(0), f.beside(1), f.beyond(0), f.beyond(1), *(g.corners() if G_DIRECT + F_DIRECT else ())))

    g_load.wait()
    g.strip(0).start()
    g.strip(1).start()
    for j in range(len(G_SIZES)):
        g.send(j)
    f_load.wait()
    f.strip(0).start()
    f.strip(1).start()
    f.send(0)

    for i in range(3):
        ft[:, 640 * i : 640 * (i + 1)] = fx[ROWS + 4 * i : ROWS + 4 * (i + 1), 16:176, :].reshape(640, 256).T
    w_load.wait()
    for kb in range(3):
        for si in range(3):
            at = (3 * kb + si) * 128
            w9[:, at : at + 128] = w[2 - kb, 2 - si]

    above, below = row > 0, row < BLOCKS - 1

    def kernel_gradient(kb, i):
        pairs = gim[kb * ROWS + 4 * i : kb * ROWS + 4 * (i + 1)].reshape(640, 384)
        products = jnp.dot(ft[:, 640 * i : 640 * (i + 1)], pairs, preferred_element_type=jnp.float32)
        for si in range(3):
            tap = products[:, si * 128 : (si + 1) * 128]
            rows = slice((2 - si) * 256, (3 - si) * 256)
            partial[2 - kb, rows, :] = tap if i == 0 else partial[2 - kb, rows, :] + tap

    def convolve(kb, first, n):
        piece = fim[kb * ROWS + first : kb * ROWS + first + n].reshape(n * 160, 768)
        return jnp.dot(piece, w[kb].reshape(768, 128), preferred_element_type=jnp.float32)

    def input_gradient(i):
        n = 4
        piece = jnp.concatenate(
            [gim[kb * ROWS + n * i : kb * ROWS + n * (i + 1)].reshape(n * 160, 384) for kb in range(3)], axis=1
        )
        grad = lax.dot_general(piece, w9[...], (((1,), (1,)), ((), ())), preferred_element_type=jnp.float32)
        back[n * i : n * (i + 1)] = grad.astype(back.dtype).reshape(n, 160, 256)

    def features_taken(j):
        f.take(0, j)
        f.take(1, j)

    def features_used(j):
        n, first = f.sizes[j], f.starts[j]
        f.took(0, j)
        f.took(1, j)
        f.unfold(fim, first, n, above)
        f.unfold(fim, 2 * ROWS + first, n, below)
        at = first * 160
        value = acc[at : at + n * 160, :] + convolve(0, first, n) + convolve(2, first, n)
        out[first : first + n] = value.astype(out.dtype).reshape(n, 160, 128)

    def cotangent_used(i):
        for way, kb, inside in ((0, 0, above), (1, 2, below)):
            g.took(way, i)
            g.unfold(gim, kb * ROWS + 4 * i, 4, inside)
            kernel_gradient(kb, i)
            if i == len(G_SIZES) - 1:
                red[2 - kb].to_core()

    def cotangent_taken(i):
        g.take(0, i)
        g.take(1, i)

    g.strip(0).wait_recv()
    g.strip(1).wait_recv()
    g.unfold(gim, ROWS, ROWS)
    for i in range(3):
        kernel_gradient(1, i)
    red[1].to_core()
    f.strip(0).wait_recv()
    f.strip(1).wait_recv()
    f.unfold(fim, ROWS, ROWS)
    acc[0:640, :] = convolve(1, 0, 4)
    red[1].to_first()
    cotangent_taken(0)
    acc[640:1280, :] = convolve(1, 4, 4)
    acc[1280:1920, :] = convolve(1, 8, 4)
    cotangent_taken(1)
    cotangent_used(0)
    red[1].to_second()
    cotangent_used(1)
    cotangent_taken(2)
    cotangent_used(2)
    red[1].to_y()
    f.send(1)
    input_gradient(0)
    red[2].to_first()
    red[0].to_first()
    features_taken(0)
    red[1].gather_parts(scale)
    input_gradient(1)
    features_used(0)
    red[2].to_second()
    red[0].to_second()
    f.send(2)
    red[1].gather_whole()
    features_taken(1)
    input_gradient(2)
    features_used(1)
    red[2].to_y()
    red[0].to_y()
    f.send(3)
    features_taken(2)
    red[1].gather_core()
    features_used(2)
    red[2].gather_parts(scale)
    red[0].gather_parts(scale)
    f.send(4)
    f.send(5)
    for d in (1, 7, 2, 6):
        red[2].take_part(d)
        red[0].take_part(d)
    features_taken(3)
    for d in (3, 5, 4):
        red[2].take_part(d)
        red[0].take_part(d)
    red[2].far_copy(0).start()
    red[0].far_copy(0).start()
    features_used(3)
    features_taken(4)
    red[2].gather_core()
    red[0].gather_core()
    features_used(4)
    features_taken(5)
    features_used(5)
    for k in (1, 2, 0):
        red[k].finish()
    for k in (1, 2, 0):
        red[k].drain()
    g.drain()
    f.drain()


def store_kernel(a, b, c, a_out, b_out, c_out, sem):
    copies = [pltpu.make_async_copy(src, dst, sem.at[i]) for i, (src, dst) in enumerate(((c, c_out), (b, b_out), (a, a_out)))]
    for copy in copies:
        copy.start()
    for copy in copies:
        copy.wait()


def stored(arrays):
    anywhere = pl.BlockSpec(memory_space=pl.ANY)
    return pl.pallas_call(
        store_kernel,
        out_shape=tuple(jax.ShapeDtypeStruct(x.shape, x.dtype) for x in arrays),
        in_specs=[anywhere] * 3,
        out_specs=(anywhere,) * 3,
        scratch_shapes=[pltpu.SemaphoreType.DMA((3,))],
        compiler_params=pltpu.CompilerParams(vmem_limit_bytes=1024 * 1024),
        name="store_kernel",
    )(*arrays)


def body(features, weight, cotangent):
    bf16, f32 = jnp.bfloat16, jnp.float32
    dma = pltpu.SemaphoreType.DMA
    pixels = ROWS * BLOCKS * 160 * COLS
    anywhere = pl.BlockSpec(memory_space=pl.ANY)
    vmem = pl.BlockSpec(memory_space=pltpu.VMEM)
    conv_out, input_grad, weight_grad = pl.pallas_call(
        functools.partial(branch_kernel, float(pixels) ** -0.5),
        out_shape=(
            jax.ShapeDtypeStruct((ROWS, 160, 128), bf16),
            jax.ShapeDtypeStruct((ROWS, 160, 256), bf16),
            jax.ShapeDtypeStruct((3, 768, 128), f32),
        ),
        in_specs=[anywhere] * 3,
        out_specs=(vmem, vmem, vmem),
        scratch_shapes=[
            pltpu.VMEM((3 * ROWS, 192, 256), bf16),
            pltpu.VMEM((3 * ROWS, 192, 128), bf16),
            pltpu.VMEM((3 * ROWS, 160, 768), bf16),
            pltpu.VMEM((3 * ROWS, 160, 384), bf16),
            pltpu.VMEM((256, ROWS * 160), bf16),
            pltpu.VMEM((3, 3, 256, 128), bf16),
            pltpu.VMEM((256, 1152), bf16),
            pltpu.VMEM((ROWS * 160, 128), f32),
            pltpu.VMEM((3, 768, 128), f32),
            dma((3,)),
            dma((2, 2)),
            dma((2, 2, len(F_SIZES))),
            dma((2, 2, 2, len(F_SIZES))),
            dma((2, 2)),
            dma((2, 2, len(G_SIZES))),
            dma((2, 2, 2, len(G_SIZES))),
        ]
        + reduction_scratch(3),
        compiler_params=pltpu.CompilerParams(collective_id=0, has_side_effects=True, vmem_limit_bytes=VMEM_BYTES),
        name="branch_kernel",
    )(*(pltpu.with_memory_space_constraint(x, pltpu.HBM) for x in (features, weight, cotangent)))
    conv_out, input_grad, weight_grad = stored((conv_out, input_grad, weight_grad))
    return conv_out, input_grad, weight_grad.reshape(weight.shape)


def solution(mesh):
    placed = (P("rows", "cols", None), P(), P("rows", "cols", None))
    return jax.shard_map(
        body,
        mesh=mesh,
        in_specs=placed,
        out_specs=(P("rows", "cols", None), P("rows", "cols", None), P()),
        check_vma=False,
    )
```

```python
import functools

import jax
import jax.numpy as jnp
from jax import lax
from jax.experimental import pallas as pl
from jax.experimental.pallas import tpu as pltpu
from jax.sharding import PartitionSpec as P

ROWS = 12
BLOCKS, COLS = 32, 8
G_SIZES, F_SIZES = (4, 4, 4), (2, 4, 2, 2, 1, 1)
G_DIRECT, F_DIRECT = 1, 1
VMEM_BYTES = 36 * 1024 * 1024
MESH = pl.DeviceIdType.MESH
NX, NY, NZ = 4, 4, 8
HALF, PART = 384, 16


def position():
    row, col = lax.axis_index("rows"), lax.axis_index("cols")
    return row, col, lax.div(col, 2), lax.rem(col, 2), lax.rem(row, NY), lax.div(row, NY)


def part_offset(i):
    return pl.multiple_of(lax.div(3 * i, 2) * 8, 8)


def rows_at(start, size):
    return pl.ds(pl.multiple_of(start, 8), size)


class Reduction:
    def __init__(self, piece, order, where, partial, total, scratch):
        self.k = piece
        self.row, self.col, self.x, self.core, self.y, self.z = where
        (self.half, self.s1, self.first, self.s2, self.second, self.ys, self.near, self.first_sem, self.second_sem,
         self.ysem, self.parts_sem, self.whole_sem, self.far_sem) = scratch
        self.partial, self.total = partial, total
        self.order = order
        self.n1, self.n2 = (NX, NZ) if order == "xz" else (NZ, NX)
        self.i1, self.i2 = (self.x, self.z) if order == "xz" else (self.z, self.x)
        self.shard = HALF // self.n1

    def copy(self, src, dst, sems, slot, to):
        return pltpu.make_async_remote_copy(
            src_ref=src, dst_ref=dst, send_sem=sems.at[0, self.k, slot], recv_sem=sems.at[1, self.k, slot], device_id=to,
            device_id_type=MESH,
        )

    def partner(self):
        return (self.row, self.x * 2 + 1 - self.core)

    def along(self, axis, d):
        if axis == "x":
            return (self.row, lax.rem(self.x + d, NX) * 2 + self.core)
        if axis == "y":
            return (self.z * NY + lax.rem(self.y + d, NY), self.col)
        return (lax.rem(self.z + d, NZ) * NY + self.y, self.col)

    def core_copy(self):
        k = self.k
        return self.copy(self.partial.at[k, rows_at((1 - self.core) * HALF, HALF)], self.half.at[k], self.near, 0, self.partner())

    def first_copy(self, d):
        k = self.k
        target = lax.rem(self.i1 + d, self.n1)
        return self.copy(
            self.s1.at[k, rows_at(target * self.shard, self.shard)], self.first.at[k, d - 1, pl.ds(0, self.shard)], self.first_sem,
            d - 1, self.along(self.order[0], d),
        )

    def second_copy(self, d):
        k = self.k
        target = lax.rem(self.i2 + d, self.n2)
        return self.copy(
            self.s2.at[k, pl.ds(part_offset(target), PART)], self.second.at[k, d - 1], self.second_sem, d - 1,
            self.along(self.order[1], d),
        )

    def y_copy(self, d):
        return self.copy(self.ys.at[self.k, self.y], self.ys.at[self.k, self.y], self.ysem, d - 1, self.along("y", d))

    def parity(self, z, body):
        even = lax.rem(z, 2) == 0
        pl.when(even)(lambda: body(0, 16))
        pl.when(jnp.logical_not(even))(lambda: body(16, 8))

    def part_of(self, z, start, size):
        base = self.core * HALF + self.i1 * self.shard + lax.div(z, 2) * 24
        return self.total.at[self.k, rows_at(base + start, size)]

    def part_copies(self, d, act):
        def go(start, size):
            here = self.part_of(self.i2, start, size)
            act(self.copy(here, here, self.parts_sem, d - 1, self.along("z", d)))

        self.parity(self.i2, go)

    def take_part(self, d):
        source = lax.rem(self.i2 + NZ - d, NZ)

        def go(start, size):
            here = self.part_of(source, start, size)
            if not isinstance(d, int) or d:
                self.copy(here, here, self.parts_sem, d - 1, self.along("z", d)).wait_recv()
            for step in (1, 3, 2):
                self.copy(here, here, self.whole_sem, step - 1, self.along("x", step)).start()

        self.parity(source, go)

    def span(self, i):
        return self.total.at[self.k, rows_at(self.core * HALF + i * self.shard, self.shard)]

    def whole_copy(self, d):
        here = self.span(self.i1)
        return self.copy(here, here, self.whole_sem, d - 1, self.along(self.order[0], d))

    def far_copy(self, d):
        here = self.span(lax.rem(self.i1 + self.n1 - d, self.n1))
        return self.copy(here, here, self.far_sem, d, self.partner())

    def loop(self, n, body, start=1):
        if n <= 4:
            for d in range(start, n):
                body(d)
            return

        def step(d, carry):
            body(d)
            return carry

        lax.fori_loop(start, n, step, 0)

    def to_core(self):
        self.core_copy().start()

    def to_first(self):
        k = self.k
        self.core_copy().wait_recv()
        self.s1[k] = self.partial[k, rows_at(self.core * HALF, HALF)] + self.half[k]
        self.loop(self.n1, lambda d: self.first_copy(d).start())

    def to_second(self):
        k, n = self.k, self.shard
        self.loop(self.n1, lambda d: self.first_copy(d).wait_recv())
        value = self.s1[k, rows_at(self.i1 * n, n)]
        for d in range(self.n1 - 1):
            value = value + self.first[k, d, 0:n]
        self.s2[k, 0:n] = value
        self.loop(self.n2, lambda d: self.second_copy(d).start())

    def to_y(self):
        k = self.k
        self.loop(self.n2, lambda d: self.second_copy(d).wait_recv())
        mine = self.s2[k, pl.ds(part_offset(self.i2), PART)]
        for d in range(self.n2 - 1):
            mine = mine + self.second[k, d]
        self.ys[k, self.y] = mine
        for d in range(1, NY):
            self.y_copy(d).start()

    def gather_parts(self, scale):
        k = self.k
        for d in range(1, NY):
            self.y_copy(d).wait_recv()
        mine = (self.ys[k, 0] + self.ys[k, 1] + self.ys[k, 2] + self.ys[k, 3]) * scale
        base = self.core * HALF + self.i1 * self.shard + lax.div(self.i2, 2) * 24

        def keep(start, size):
            self.total[k, rows_at(base + start, size)] = mine[16 - size :]

        self.parity(self.i2, keep)
        self.loop(NZ, lambda d: self.part_copies(d, lambda copy: copy.start()))
        self.take_part(0)

    def gather_whole(self):
        for d in (1, 7, 2, 6, 3, 5, 4):
            self.take_part(d)
        self.far_copy(0).start()

    def gather_core(self):
        def hand_on(d):
            self.whole_copy(d).wait_recv()
            self.far_copy(d).start()

        self.loop(self.n1, hand_on)

    def finish(self):
        self.loop(self.n1, lambda d: self.far_copy(d).wait_recv(), 0)

    def drain(self):
        self.core_copy().wait_send()
        self.loop(self.n1, lambda d: self.first_copy(d).wait_send())
        self.loop(self.n1, lambda d: self.whole_copy(d).wait_send())
        self.loop(self.n2, lambda d: self.second_copy(d).wait_send())
        self.loop(NZ, lambda d: self.part_copies(d, lambda copy: copy.wait_send()))
        for d in range(1, NY):
            self.y_copy(d).wait_send()
        self.loop(self.n1, lambda d: self.far_copy(d).wait_send(), 0)


def reduction_scratch(pieces):
    f32 = jnp.float32
    dma = pltpu.SemaphoreType.DMA
    most = max(NX, NZ)
    return [
        pltpu.VMEM((pieces, HALF, 128), f32),
        pltpu.VMEM((pieces, HALF, 128), f32),
        pltpu.VMEM((pieces, most - 1, HALF // NX, 128), f32),
        pltpu.VMEM((pieces, HALF // NX, 128), f32),
        pltpu.VMEM((pieces, most - 1, PART, 128), f32),
        pltpu.VMEM((pieces, NY, PART, 128), f32),
        dma((2, pieces, 1)),
        dma((2, pieces, most - 1)),
        dma((2, pieces, most - 1)),
        dma((2, pieces, NY - 1)),
        dma((2, pieces, most - 1)),
        dma((2, pieces, most - 1)),
        dma((2, pieces, most)),
    ]


def greet(where, extra=()):
    row, col, x, core, y, z = where
    barrier = pltpu.get_barrier_semaphore()

    def signal(to):
        pl.semaphore_signal(barrier, inc=1, device_id=to, device_id_type=MESH)

    count = 0
    for to in extra:
        signal(to)
        count += 1
    signal((row, x * 2 + 1 - core))
    for d in range(1, NX):
        signal((row, lax.rem(x + d, NX) * 2 + core))
    for d in range(1, NY):
        signal((z * NY + lax.rem(y + d, NY), col))

    def step(d, carry):
        signal((lax.rem(z + d, NZ) * NY + y, col))
        return carry

    lax.fori_loop(1, NZ, step, 0)
    pl.semaphore_wait(barrier, count + 1 + NX - 1 + NY - 1 + NZ - 1)


class Halo:
    def __init__(self, buf, where, strip_sem, row_sem, relay_sem, sizes, direct=0):
        self.buf = buf
        self.row, self.col = where[0], where[1]
        self.strip_sem, self.row_sem, self.relay_sem = strip_sem, row_sem, relay_sem
        self.sizes = sizes
        self.starts = [sum(sizes[:j]) for j in range(len(sizes))]
        self.chunks = len(sizes)
        self.relayed = self.chunks - direct

    def beside(self, side):
        step = 1 if side == 1 else COLS - 1
        return (self.row, lax.rem(self.col + step, COLS))

    def beyond(self, way):
        step = 1 if way == 0 else BLOCKS - 1
        return (lax.rem(self.row + step, BLOCKS), self.col)

    def edge(self, side):
        return (pl.ds(160, 16), pl.ds(0, 16)) if side == 1 else (pl.ds(16, 16), pl.ds(176, 16))

    def copy(self, src, dst, send, recv, to):
        return pltpu.make_async_remote_copy(
            src_ref=src, dst_ref=dst, send_sem=send, recv_sem=recv, device_id=to, device_id_type=MESH
        )

    def strip(self, side):
        here, there = self.edge(side)
        rows = pl.ds(ROWS, ROWS)
        return self.copy(
            self.buf.at[rows, here, :], self.buf.at[rows, there, :], self.strip_sem.at[0, side], self.strip_sem.at[1, side],
            self.beside(side),
        )

    def block(self, way, j):
        src = pl.ds(ROWS + self.starts[j], self.sizes[j])
        dst = pl.ds((0 if way == 0 else 2 * ROWS) + self.starts[j], self.sizes[j])
        mid = pl.ds(16, 160)
        return self.copy(
            self.buf.at[src, mid, :], self.buf.at[dst, mid, :], self.row_sem.at[0, way, j], self.row_sem.at[1, way, j], self.beyond(way)
        )

    def relay(self, way, side, j):
        here, there = self.edge(side)
        rows = pl.ds((0 if way == 0 else 2 * ROWS) + self.starts[j], self.sizes[j])
        source, to = rows, self.beside(side)
        if j >= self.relayed:
            source, to = pl.ds(ROWS + self.starts[j], self.sizes[j]), (self.beyond(way)[0], self.beside(side)[1])
        return self.copy(
            self.buf.at[source, here, :], self.buf.at[rows, there, :], self.relay_sem.at[0, way, side, j],
            self.relay_sem.at[1, way, side, j], to,
        )

    def send(self, j):
        if j >= self.relayed:
            for way in range(2):
                for side in range(2):
                    self.relay(way, side, j).start()
        for way in range(2):
            self.block(way, j).start()

    def corners(self):
        return [(self.beyond(way)[0], self.beside(side)[1]) for way in range(2) for side in range(2)]

    def take(self, way, j):
        self.block(way, j).wait_recv()
        if j < self.relayed:
            self.relay(way, 0, j).start()
            self.relay(way, 1, j).start()

    def took(self, way, j):
        self.relay(way, 0, j).wait_recv()
        self.relay(way, 1, j).wait_recv()

    def blank_columns(self, first, n):
        zeros = jnp.zeros((n, 16, self.buf.shape[2]), self.buf.dtype)

        @pl.when(self.col == 0)
        def _():
            self.buf[first : first + n, 0:16, :] = zeros

        @pl.when(self.col == COLS - 1)
        def _():
            self.buf[first : first + n, 176:192, :] = zeros

    def unfold(self, into, first, n, inside=None):
        c = self.buf.shape[2]
        self.blank_columns(first, n)

        def shift():
            def body(i, carry):
                r = first + i
                into[r, :, 0:c] = self.buf[r, 4:164, :]
                into[r, :, c : 2 * c] = self.buf[r, 16:176, :]
                into[r, :, 2 * c : 3 * c] = self.buf[r, 28:188, :]
                return carry

            lax.fori_loop(0, n, body, 0)

        if inside is None:
            shift()
            return
        pl.when(inside)(shift)

        @pl.when(jnp.logical_not(inside))
        def _():
            def body(i, carry):
                into[first + i] = jnp.zeros((160, 3 * c), into.dtype)
                return carry

            lax.fori_loop(0, n, body, 0)

    def drain(self):
        for side in range(2):
            self.strip(side).wait_send()
        for way in range(2):
            for j in range(self.chunks):
                self.block(way, j).wait_send()
                for side in range(2):
                    self.relay(way, side, j).wait_send()


def branch_kernel(scale, f_hbm, w_hbm, g_hbm, out, back, total, *scratch):
    (fx, gx, fim, gim, ft, w, w9, acc, partial, load_sem, f_strip, f_row, f_relay, g_strip, g_row, g_relay) = scratch[:16]
    where = position()
    row, col = where[0], where[1]
    mine = pl.ds(ROWS, ROWS)
    g_load = pltpu.make_async_copy(g_hbm, gx.at[mine, pl.ds(16, 160), :], load_sem.at[0])
    f_load = pltpu.make_async_copy(f_hbm, fx.at[mine, pl.ds(16, 160), :], load_sem.at[1])
    w_load = pltpu.make_async_copy(w_hbm, w, load_sem.at[2])
    g_load.start()
    f_load.start()
    w_load.start()
    f = Halo(fx, where, f_strip, f_row, f_relay, F_SIZES, F_DIRECT)
    g = Halo(gx, where, g_strip, g_row, g_relay, G_SIZES, G_DIRECT)
    red = [Reduction(k, order, where, partial, total, scratch[16:]) for k, order in enumerate(("xz", "xz", "xz"))]
    greet(where, (f.beside(0), f.beside(1), f.beyond(0), f.beyond(1), *(g.corners() if G_DIRECT + F_DIRECT else ())))

    g_load.wait()
    g.strip(0).start()
    g.strip(1).start()
    for j in range(len(G_SIZES)):
        g.send(j)
    f_load.wait()
    f.strip(0).start()
    f.strip(1).start()
    f.send(0)

    for i in range(3):
        ft[:, 640 * i : 640 * (i + 1)] = fx[ROWS + 4 * i : ROWS + 4 * (i + 1), 16:176, :].reshape(640, 256).T
    w_load.wait()
    for kb in range(3):
        for si in range(3):
            at = (3 * kb + si) * 128
            w9[:, at : at + 128] = w[2 - kb, 2 - si]

    above, below = row > 0, row < BLOCKS - 1

    def kernel_gradient(kb, i):
        pairs = gim[kb * ROWS + 4 * i : kb * ROWS + 4 * (i + 1)].reshape(640, 384)
        products = jnp.dot(ft[:, 640 * i : 640 * (i + 1)], pairs, preferred_element_type=jnp.float32)
        for si in range(3):
            tap = products[:, si * 128 : (si + 1) * 128]
            rows = slice((2 - si) * 256, (3 - si) * 256)
            partial[2 - kb, rows, :] = tap if i == 0 else partial[2 - kb, rows, :] + tap

    def convolve(kb, first, n):
        piece = fim[kb * ROWS + first : kb * ROWS + first + n].reshape(n * 160, 768)
        return jnp.dot(piece, w[kb].reshape(768, 128), preferred_element_type=jnp.float32)

    def input_gradient(i):
        n = 4
        piece = jnp.concatenate(
            [gim[kb * ROWS + n * i : kb * ROWS + n * (i + 1)].reshape(n * 160, 384) for kb in range(3)], axis=1
        )
        grad = lax.dot_general(piece, w9[...], (((1,), (1,)), ((), ())), preferred_element_type=jnp.float32)
        back[n * i : n * (i + 1)] = grad.astype(back.dtype).reshape(n, 160, 256)

    def features_taken(j):
        f.take(0, j)
        f.take(1, j)

    def features_used(j):
        n, first = f.sizes[j], f.starts[j]
        f.took(0, j)
        f.took(1, j)
        f.unfold(fim, first, n, above)
        f.unfold(fim, 2 * ROWS + first, n, below)
        at = first * 160
        value = acc[at : at + n * 160, :] + convolve(0, first, n) + convolve(2, first, n)
        out[first : first + n] = value.astype(out.dtype).reshape(n, 160, 128)

    def cotangent_used(i):
        for way, kb, inside in ((0, 0, above), (1, 2, below)):
            g.took(way, i)
            g.unfold(gim, kb * ROWS + 4 * i, 4, inside)
            kernel_gradient(kb, i)
            if i == len(G_SIZES) - 1:
                red[2 - kb].to_core()

    def cotangent_taken(i):
        g.take(0, i)
        g.take(1, i)

    g.strip(0).wait_recv()
    g.strip(1).wait_recv()
    g.unfold(gim, ROWS, ROWS)
    for i in range(3):
        kernel_gradient(1, i)
    red[1].to_core()
    f.strip(0).wait_recv()
    f.strip(1).wait_recv()
    f.unfold(fim, ROWS, ROWS)
    acc[0:640, :] = convolve(1, 0, 4)
    red[1].to_first()
    cotangent_taken(0)
    acc[640:1280, :] = convolve(1, 4, 4)
    acc[1280:1920, :] = convolve(1, 8, 4)
    cotangent_taken(1)
    cotangent_used(0)
    red[1].to_second()
    cotangent_used(1)
    cotangent_taken(2)
    cotangent_used(2)
    red[1].to_y()
    f.send(1)
    input_gradient(0)
    red[2].to_first()
    red[0].to_first()
    features_taken(0)
    red[1].gather_parts(scale)
    input_gradient(1)
    features_used(0)
    red[2].to_second()
    red[0].to_second()
    f.send(2)
    red[1].gather_whole()
    features_taken(1)
    input_gradient(2)
    features_used(1)
    red[2].to_y()
    red[0].to_y()
    f.send(3)
    features_taken(2)
    red[1].gather_core()
    features_used(2)
    red[2].gather_parts(scale)
    red[0].gather_parts(scale)
    f.send(4)
    f.send(5)
    for d in (1, 7, 2, 6):
        red[2].take_part(d)
        red[0].take_part(d)
    features_taken(3)
    for d in (3, 5, 4):
        red[2].take_part(d)
        red[0].take_part(d)
    red[2].far_copy(0).start()
    red[0].far_copy(0).start()
    features_used(3)
    features_taken(4)
    red[2].gather_core()
    red[0].gather_core()
    features_used(4)
    features_taken(5)
    features_used(5)
    for k in (1, 2, 0):
        red[k].finish()
    for k in (1, 2, 0):
        red[k].drain()
    g.drain()
    f.drain()


def store_kernel(a, b, c, a_out, b_out, c_out, sem):
    copies = [pltpu.make_async_copy(src, dst, sem.at[i]) for i, (src, dst) in enumerate(((c, c_out), (b, b_out), (a, a_out)))]
    for copy in copies:
        copy.start()
    for copy in copies:
        copy.wait()


def stored(arrays):
    anywhere = pl.BlockSpec(memory_space=pl.ANY)
    return pl.pallas_call(
        store_kernel,
        out_shape=tuple(jax.ShapeDtypeStruct(x.shape, x.dtype) for x in arrays),
        in_specs=[anywhere] * 3,
        out_specs=(anywhere,) * 3,
        scratch_shapes=[pltpu.SemaphoreType.DMA((3,))],
        compiler_params=pltpu.CompilerParams(vmem_limit_bytes=1024 * 1024),
        name="store_kernel",
    )(*arrays)


def body(features, weight, cotangent):
    bf16, f32 = jnp.bfloat16, jnp.float32
    dma = pltpu.SemaphoreType.DMA
    pixels = ROWS * BLOCKS * 160 * COLS
    anywhere = pl.BlockSpec(memory_space=pl.ANY)
    vmem = pl.BlockSpec(memory_space=pltpu.VMEM)
    conv_out, input_grad, weight_grad = pl.pallas_call(
        functools.partial(branch_kernel, float(pixels) ** -0.5),
        out_shape=(
            jax.ShapeDtypeStruct((ROWS, 160, 128), bf16),
            jax.ShapeDtypeStruct((ROWS, 160, 256), bf16),
            jax.ShapeDtypeStruct((3, 768, 128), f32),
        ),
        in_specs=[anywhere] * 3,
        out_specs=(vmem, vmem, vmem),
        scratch_shapes=[
            pltpu.VMEM((3 * ROWS, 192, 256), bf16),
            pltpu.VMEM((3 * ROWS, 192, 128), bf16),
            pltpu.VMEM((3 * ROWS, 160, 768), bf16),
            pltpu.VMEM((3 * ROWS, 160, 384), bf16),
            pltpu.VMEM((256, ROWS * 160), bf16),
            pltpu.VMEM((3, 3, 256, 128), bf16),
            pltpu.VMEM((256, 1152), bf16),
            pltpu.VMEM((ROWS * 160, 128), f32),
            pltpu.VMEM((3, 768, 128), f32),
            dma((3,)),
            dma((2, 2)),
            dma((2, 2, len(F_SIZES))),
            dma((2, 2, 2, len(F_SIZES))),
            dma((2, 2)),
            dma((2, 2, len(G_SIZES))),
            dma((2, 2, 2, len(G_SIZES))),
        ]
        + reduction_scratch(3),
        compiler_params=pltpu.CompilerParams(collective_id=0, has_side_effects=True, vmem_limit_bytes=VMEM_BYTES),
        name="branch_kernel",
    )(*(pltpu.with_memory_space_constraint(x, pltpu.HBM) for x in (features, weight, cotangent)))
    conv_out, input_grad, weight_grad = stored((conv_out, input_grad, weight_grad))
    return conv_out, input_grad, weight_grad.reshape(weight.shape)


def solution(mesh):
    placed = (P("rows", "cols", None), P(), P("rows", "cols", None))
    return jax.shard_map(
        body,
        mesh=mesh,
        in_specs=placed,
        out_specs=(P("rows", "cols", None), P("rows", "cols", None), P()),
        check_vma=False,
    )
```
